128 devices in a mesh: row: 16 (over z, x), col: 8 (over y, core).
Axes of the slice: x: 4, y: 4, z: 4, core: 2. Of those that a mesh axis runs over, the one named last changes fastest.
Arguments:
- tokens: bfloat16 [8192, 4096], P('row'), may hold values from -6 to 6
- theta: bfloat16 [96, 1024, 128], P('col', 'row'), may hold values from -0.1875 to 0.1875
- log_sigma2: float32 [96, 1024, 128], P('col', 'row'), may hold values from -8 to -5
- block_rows: int32 [96, 8], P('col'), may hold values from 0 to 31, as said below
- noise: bfloat16 [8192, 12288], P('row', 'col'), may hold values from -6 to 6
- cotangent: bfloat16 [8192, 12288], P('row', 'col'), may hold values from -6 to 6
Outputs:
- output: bfloat16 [8192, 12288], P('row', 'col')
- grad_tokens: float32 [8192, 4096], P('row', 'col')
- grad_theta: float32 [96, 1024, 128], P('col', 'row')
- grad_logvar: float32 [96, 1024, 128], P('col', 'row')
The draws below stay inside these ranges and needn't reach their ends.
Inputs may be any that keep to these rules, and one draw needn't show every extreme that they name: `block_rows`: each row lists 8 distinct block rows in increasing order; row n contains n modulo 32, the others are drawn uniformly.
All inputs are finite; a program needn't handle non-finite values.
Results may differ from the reference program's by a relative error of at most 0.014.
Values may be sent and summed in bfloat16 or wider, within the bound.
No kernel may reach another device: no remote copies, remote signals or barrier semaphores. Data moves between devices by JAX's collectives and lax.ppermute only.
A program may use at most 192 MiB of HBM per device.

```python
import math
import jax
import jax.numpy as jnp
from jax import lax

D = 4096
FF = 12288
BLK = 128
TOK_ROW = 512
TOKENS = 8192
KB = 32
NB = 96
KS = 8
N_ROW = 16
N_COL = 8


def draw_block_rows(key, part):
    keys = jax.random.split(key, NB)
    ranks = jax.vmap(lambda one: jax.random.permutation(one, KB))(keys).astype(jnp.int32)
    forced = (jnp.arange(NB, dtype=jnp.int32) % KB)[:, None]
    places = jnp.arange(KB, dtype=jnp.int32)[None, :]
    ranks = jnp.where(places == forced, -1, ranks)
    order = jnp.argsort(ranks, axis=1, stable=True)[:, :KS]
    return jnp.sort(order, axis=1).astype(jnp.int32)


def level_of(own_key, dims, cuts, low, high):
    gain, own = 1.0, jax.random.fold_in(own_key, 6)
    for position, blocks in cuts:
        heights = jnp.exp(jax.random.uniform(jax.random.fold_in(own, position), (blocks,), jnp.float32, low / len(cuts), high / len(cuts)))
        gain = gain * jnp.repeat(heights, dims[position] // blocks).reshape([-1 if axis == position else 1 for axis in range(len(dims))])
    return gain


def centred(own_key, shape, deviation, reach, shards=(), kind=jnp.bfloat16):
    values = jax.random.normal(own_key, shape, jnp.float32) * deviation
    if len(shards) > 0:
        values = level_of(own_key, shape, shards, -0.22, 0.18) * values
    return jnp.clip(values, min=-reach, max=reach).astype(kind)


def setup_inputs(seed: int = 0) -> dict:
    key_of = jax.random.split(jax.random.key(seed), 7)
    tokens = centred(key_of[0], (TOKENS, D), 1.0, 6.0, ((0, 16),))
    theta = centred(key_of[1], (NB, KS * BLK, BLK), (KS * BLK) ** -0.5, 0.1875, ((0, 8), (1, 16)))
    log_sigma2 = jnp.clip(-8.0 + 3.0 * jax.random.uniform(key_of[2], (NB, KS * BLK, BLK), jnp.float32) ** level_of(key_of[2], (NB, KS * BLK, BLK), ((0, 8), (1, 16)), -0.2, 0.2), -8.0, -5.0)
    block_rows = draw_block_rows(jax.random.fold_in(key_of[6], 71), 0)
    noise = centred(key_of[4], (TOKENS, FF), 1.0, 6.0, ((0, 16), (1, 8)))
    cotangent = centred(key_of[5], (TOKENS, FF), 1.0, 6.0, ((0, 16), (1, 8)))
    return dict(tokens=tokens, theta=theta, log_sigma2=log_sigma2, block_rows=block_rows, noise=noise, cotangent=cotangent)


EPS = 1e-06

def squares_of(values):
    wide = values.astype(jnp.float32)
    return (wide * wide).astype(jnp.bfloat16)

def row_partials(left, right):
    first = left.reshape(N_ROW, TOK_ROW, left.shape[1]).astype(jnp.float32)
    second = right.reshape(N_ROW, TOK_ROW, right.shape[1]).astype(jnp.float32)
    parts = jnp.einsum('rtk,rtj->rkj', first, second, precision=lax.Precision.HIGHEST)
    rounded = lax.optimization_barrier(parts.astype(jnp.bfloat16))
    return lax.optimization_barrier(jnp.sum(rounded.astype(jnp.float32), axis=0))

def reference(tokens, theta, log_sigma2, block_rows, noise, cotangent):
    sigma = jnp.exp(log_sigma2)
    sigma_low = sigma.astype(jnp.bfloat16)
    tiles = tokens.reshape(TOKENS, KB, BLK)
    slab = NB // N_COL
    width = KS * BLK
    inv_root = 1.0 / math.sqrt(TOKENS)
    var_scale = width / math.sqrt(TOKENS)

    def column(dx_acc, index):
        rows = block_rows[index]
        panel = jnp.take(tiles, rows, axis=1).reshape(TOKENS, width)
        sq_panel = squares_of(panel)
        weight = theta[index]
        spread = sigma_low[index]
        mean_out = jnp.dot(panel, weight, preferred_element_type=jnp.float32)
        var_out = jnp.dot(sq_panel, spread, preferred_element_type=jnp.float32)
        root = jnp.sqrt(var_out + EPS)
        draw = lax.dynamic_slice_in_dim(noise, index * BLK, BLK, 1).astype(jnp.float32)
        grad = lax.dynamic_slice_in_dim(cotangent, index * BLK, BLK, 1)
        result = (mean_out + root * draw).astype(jnp.bfloat16)
        grad_var = (grad.astype(jnp.float32) * draw / (2.0 * root)).astype(jnp.bfloat16)
        g_theta = row_partials(panel, grad) * inv_root
        g_var = sigma[index] * row_partials(sq_panel, grad_var) * var_scale
        back = jnp.dot(grad, weight.T, preferred_element_type=jnp.float32)
        back = back + 2.0 * panel.astype(jnp.float32) * jnp.dot(grad_var, spread.T, preferred_element_type=jnp.float32)
        dx_acc = dx_acc.at[:, rows].add(back.reshape(TOKENS, KS, BLK))
        return (dx_acc, (result, g_theta, g_var))

    def one_slab(total, slab_index):
        indices = slab_index * slab + jnp.arange(slab, dtype=jnp.int32)
        start = jnp.zeros((TOKENS, KB, BLK), jnp.float32)
        dx_part, pieces = lax.scan(column, start, indices)
        rounded = lax.optimization_barrier(dx_part.reshape(TOKENS, D).astype(jnp.bfloat16))
        return (total + rounded.astype(jnp.float32), pieces)
    begin = jnp.zeros((TOKENS, D), jnp.float32)
    total, stacked = lax.scan(one_slab, begin, jnp.arange(N_COL, dtype=jnp.int32))
    results, g_thetas, g_vars = stacked
    output = results.reshape(NB, TOKENS, BLK).transpose(1, 0, 2).reshape(TOKENS, FF)
    grad_theta = g_thetas.reshape(NB, width, BLK)
    grad_logvar = g_vars.reshape(NB, width, BLK)
    return (output, total, grad_theta, grad_logvar)
```

```python
import math
import jax, jax.numpy as jnp
from jax import lax
from jax.experimental import pallas as pl
from jax.experimental.pallas import tpu as pltpu
from jax.sharding import Mesh
from jax.sharding import PartitionSpec as P

ROW = ("row_0", "row_1")

EPS = 1e-06
VM = pltpu.CompilerParams(vmem_limit_bytes=60 * 1024 * 1024)
f32, bf16 = jnp.float32, jnp.bfloat16

def lanes(ref, index, rows=slice(None)):
    return ref[rows, pl.ds(pl.multiple_of(index * 128, 128), 128)]

def tiles_of(ref, rows_ref, n, count):
    return [ref.at[:, pl.ds(pl.multiple_of(rows_ref[n, s] * 128, 128), 128)] for s in range(count)]

def prep_kernel(theta_ref, ls_ref, th_ref, sg_ref):
    for n in range(theta_ref.shape[0]):
        th_ref[:, n * 128:(n + 1) * 128] = theta_ref[n]
        sg_ref[:, n * 128:(n + 1) * 128] = jnp.exp(ls_ref[n]).astype(bf16)

def prep(theta, ls):
    c, r, b = theta.shape
    o = jax.ShapeDtypeStruct((r, c * b), bf16)
    return pl.pallas_call(prep_kernel, out_shape=(o, o), compiler_params=VM, name="prep")(theta, ls)

def k1_kernel(rows_ref, tok_ref, cot_ref, part_ref, tokT_ref):
    kb = tok_ref.shape[1] // 128
    cols = cot_ref.shape[1] // 128
    ks = rows_ref.shape[1]
    for k in range(kb):
        tokT_ref[k] = tok_ref[:, k * 128:(k + 1) * 128].T
    def step(n, _):
        lhs = jnp.concatenate([tokT_ref[rows_ref[n, s]] for s in range(ks)], axis=0)
        part = jnp.dot(lhs, lanes(cot_ref, n), preferred_element_type=f32)
        part_ref[:, pl.ds(pl.multiple_of(n * 128, 128), 128)] = part.astype(bf16)
        return 0
    lax.fori_loop(0, cols, step, 0)

SM = pl.BlockSpec(memory_space=pltpu.SMEM)
VB = pl.BlockSpec(memory_space=pltpu.VMEM)

def k1(rows, tok, cot):
    t, d = tok.shape
    width = rows.shape[1] * 128
    return pl.pallas_call(k1_kernel,
        out_shape=(jax.ShapeDtypeStruct((width, cot.shape[1]), bf16), jax.ShapeDtypeStruct((d // 128, 128, t), bf16)),
        in_specs=[SM, VB, VB], out_specs=(VB, VB), compiler_params=VM, name="k1")(rows, tok, cot)

def k2_kernel(rows_ref, tok_ref, tokT_ref, sg_ref, noise_ref, cot_ref, part_ref, gv_ref, rn_ref, sq_ref, sqT_ref):
    kb = tok_ref.shape[1] // 128
    cols = cot_ref.shape[1] // 128
    ks = rows_ref.shape[1]
    for k in range(kb):
        w = tok_ref[:, k * 128:(k + 1) * 128].astype(f32)
        sq_ref[:, k * 128:(k + 1) * 128] = (w * w).astype(bf16)
        w = tokT_ref[k].astype(f32)
        sqT_ref[k] = (w * w).astype(bf16)
    def step(n, _):
        at = pl.ds(pl.multiple_of(n * 128, 128), 128)
        lhs = jnp.concatenate([lanes(sq_ref, rows_ref[n, s]) for s in range(ks)], axis=1)
        var = jnp.dot(lhs, sg_ref[:, at], preferred_element_type=f32)
        root = jnp.sqrt(var + EPS)
        draw = noise_ref[:, at].astype(f32)
        rn_ref[:, at] = root * draw
        gv = (cot_ref[:, at].astype(f32) * draw / (2.0 * root)).astype(bf16)
        gv_ref[:, at] = gv
        lhs = jnp.concatenate([sqT_ref[rows_ref[n, s]] for s in range(ks)], axis=0)
        part = jnp.dot(lhs, gv, preferred_element_type=f32)
        part_ref[:, at] = part.astype(bf16)
        return 0
    lax.fori_loop(0, cols, step, 0)

def k2(rows, tok, tokT, sg, noise, cot):
    t, d = tok.shape
    width, ff = sg.shape
    return pl.pallas_call(k2_kernel,
        out_shape=(jax.ShapeDtypeStruct((width, ff), bf16), jax.ShapeDtypeStruct((t, ff), bf16), jax.ShapeDtypeStruct((t, ff), f32)),
        in_specs=[SM, VB, VB, VB, VB, VB], out_specs=(VB, VB, VB),
        scratch_shapes=[pltpu.VMEM((t, d), bf16), pltpu.VMEM((d // 128, 128, t), bf16)],
        compiler_params=VM, name="k2")(rows, tok, tokT, sg, noise, cot)

NT = (((1,), (1,)), ((), ()))

def k3_kernel(rows_ref, tok_ref, th_ref, sg_ref, cot_ref, gv_ref, rn_ref, out_ref, dx_ref, acc_ref):
    t = tok_ref.shape[0]
    kb = tok_ref.shape[1] // 128
    cols = cot_ref.shape[1] // 128
    ks = rows_ref.shape[1]
    acc_ref[...] = jnp.zeros_like(acc_ref)
    def step(n, _):
        at = pl.ds(pl.multiple_of(n * 128, 128), 128)
        th = th_ref[:, at]
        sg = sg_ref[:, at]
        lhs = jnp.concatenate([lanes(tok_ref, rows_ref[n, s]) for s in range(ks)], axis=1)
        mean = jnp.dot(lhs, th, preferred_element_type=f32)
        out_ref[:, at] = (mean + rn_ref[:, at]).astype(bf16)
        cot = cot_ref[:, at]
        gv = gv_ref[:, at]
        first = lax.dot_general(cot, th, NT, preferred_element_type=f32)
        second = lax.dot_general(gv, sg, NT, preferred_element_type=f32)
        for s in range(ks):
            pick = pl.ds(pl.multiple_of(rows_ref[n, s] * 128, 128), 128)
            p = slice(s * 128, (s + 1) * 128)
            acc_ref[:, pick] += first[:, p] + 2.0 * tok_ref[:, pick].astype(f32) * second[:, p]
        return 0
    lax.fori_loop(0, cols, step, 0)
    w = dx_ref.shape[2]
    for c in range(dx_ref.shape[0]):
        dx_ref[c] = acc_ref[:, c * w:(c + 1) * w].astype(bf16)

def k3(rows, tok, th, sg, cot, gv, rn):
    t, d = tok.shape
    ff = cot.shape[1]
    return pl.pallas_call(k3_kernel,
        out_shape=(jax.ShapeDtypeStruct((t, ff), bf16), jax.ShapeDtypeStruct((8, t, d // 8), bf16)),
        in_specs=[SM, VB, VB, VB, VB, VB, VB], out_specs=(VB, VB),
        scratch_shapes=[pltpu.VMEM((t, d), f32)],
        compiler_params=VM, name="k3")(rows, tok, th, sg, cot, gv, rn)


def body(tokens, theta, log_sigma2, block_rows, noise, cotangent):
    th_own, sg_own = prep(theta, log_sigma2)
    sg = lax.all_gather(sg_own, ROW, axis=0, tiled=True)
    th = lax.all_gather(th_own, ROW, axis=0, tiled=True)
    part_theta, tokT = k1(block_rows, tokens, cotangent)
    part_var, gv, rn = k2(block_rows, tokens, tokT, sg, noise, cotangent)
    output, dx = k3(block_rows, tokens, th, sg, cotangent, gv, rn)
    sum_theta = lax.psum_scatter(part_theta, ROW, scatter_dimension=0, tiled=True).astype(f32)
    sum_var = lax.psum_scatter(part_var, ROW, scatter_dimension=0, tiled=True).astype(f32)
    c, r, b = theta.shape
    width = part_theta.shape[0]
    tokens_all = tokens.shape[0] * lax.axis_size(ROW)
    back = lambda v: v.reshape(r, c, b).transpose(1, 0, 2)
    grad_theta = back(sum_theta) * (1.0 / math.sqrt(tokens_all))
    grad_logvar = jnp.exp(log_sigma2) * back(sum_var) * (width / math.sqrt(tokens_all))
    arrived = lax.all_to_all(dx, "col", split_axis=0, concat_axis=0, tiled=True)
    grad_tokens = arrived.astype(f32).sum(axis=0)
    return (output, grad_tokens, grad_theta, grad_logvar)


def solution(mesh):
    finer = Mesh(mesh.devices.reshape(4, 4, mesh.shape["col"]), ("row_0", "row_1", "col"))
    in_specs = (P(ROW, None), P("col", ROW, None), P("col", ROW, None), P("col", None), P(ROW, "col"), P(ROW, "col"))
    out_specs = (P(ROW, "col"), P(ROW, "col"), P("col", ROW, None), P("col", ROW, None))
    return jax.shard_map(body, mesh=finer, in_specs=in_specs, out_specs=out_specs, check_vma=False)
```

```python
import math

import jax
import jax.numpy as jnp
from jax import lax
from jax.experimental import pallas as pl
from jax.experimental.pallas import tpu as pltpu
from jax.sharding import Mesh
from jax.sharding import PartitionSpec as P


ROW = ("z", "x")
COL = ("y", "core")
RING = 4
EPS = 1e-06
LANE = 128
f32, bf16 = jnp.float32, jnp.bfloat16
PARAMS = pltpu.CompilerParams(vmem_limit_bytes=60 * 1024 * 1024)
SM = pl.BlockSpec(memory_space=pltpu.SMEM)
VB = pl.BlockSpec(memory_space=pltpu.VMEM)
HB = pl.BlockSpec(memory_space=pl.ANY)
NT = (((1,), (1,)), ((), ()))

GATHER_SIGMA = (("x", "z", 0, 32), ("z", "x", 32, 64))
GATHER_THETA = (("x", "z", 0, 32), ("z", "x", 32, 64))
SCATTER_THETA = (("x", "z", 0, 32), ("z", "x", 32, 64))
SCATTER_VAR = (("x", "z", 0, 32), ("z", "x", 32, 64))
PLACE = {"z": 0, "x": 1, "y": 2, "core": 3}


def sds(shape, dtype):
    return jax.ShapeDtypeStruct(shape, dtype)


def at_block(index):
    return pl.ds(pl.multiple_of(index * LANE, LANE), LANE)


def sent(value, axis, step):
    n = lax.axis_size(axis)
    return lax.ppermute(value, axis, [(i, (i + step) % n) for i in range(n)])


def steps_of(value, axis):
    return [sent(value, axis, k) for k in range(1, RING)]


def prep_kernel(paths_s, paths_t):
    def kernel(ls_ref, theta_ref, *outs):
        for n in range(theta_ref.shape[0]):
            at = slice(n * LANE, (n + 1) * LANE)
            for (_, _, lo, hi), o in zip(paths_s, outs):
                o[:, at] = jnp.exp(ls_ref[n, lo:hi]).astype(bf16)
            for (_, _, lo, hi), o in zip(paths_t, outs[len(paths_s) :]):
                o[:, at] = theta_ref[n, lo:hi]

    return kernel


def prep(ls, theta):
    c, _, b = theta.shape
    shapes = [sds((hi - lo, c * b), bf16) for _, _, lo, hi in GATHER_SIGMA + GATHER_THETA]
    outs = pl.pallas_call(
        prep_kernel(GATHER_SIGMA, GATHER_THETA), out_shape=shapes, compiler_params=PARAMS, name="prep"
    )(ls, theta)
    return outs[: len(GATHER_SIGMA)], outs[len(GATHER_SIGMA) :]


def gather(pieces, paths):
    blocks = [jnp.stack([p] + steps_of(p, path[0])) for p, path in zip(pieces, paths)]
    return [[b] + steps_of(b, path[1]) for b, path in zip(blocks, paths)]


def gather_copies(place, paths, groups, whole, sem):
    copies = []
    for (one, two, lo, hi), refs in zip(paths, groups):
        for k in range(RING):
            for j in range(RING):
                spot = {one: (place[PLACE[one]] - j) & 3, two: (place[PLACE[two]] - k) & 3}
                copies.append(pltpu.make_async_copy(refs[k].at[j], whole.at[spot["z"], spot["x"], lo:hi, :], sem))
    return copies


def chunked(refs, size):
    return [refs[i : i + size] for i in range(0, len(refs), size)]


def block_column(whole, n):
    blk = whole[:, :, :, at_block(n)]
    return blk.reshape(-1, LANE)


def scatter_copies(place, paths, held, groups, sem):
    copies = []
    for (one, _, lo, hi), refs in zip(paths, groups):
        for k in range(RING):
            spot = (place[PLACE[one]] + k) & 3
            src = held.at[spot, :, lo:hi, :] if one == "z" else held.at[:, spot, lo:hi, :]
            copies.append(pltpu.make_async_copy(src, refs[k], sem))
    return copies


def scatter_shapes(paths, ff):
    return [sds((RING, hi - lo, ff), bf16) for _, _, lo, hi in paths for _ in range(RING)]


def sum_kernel(paths):
    def kernel(place, *refs):
        ins, outs = refs[: RING * len(paths)], refs[RING * len(paths) :]
        for path, arrived, left in zip(paths, chunked(ins, RING), chunked(outs, RING)):
            own = place[PLACE[path[1]]]
            for k in range(RING):
                spot = (own + k) & 3
                total = arrived[0][spot].astype(f32)
                for r in arrived[1:]:
                    total = total + r[spot].astype(f32)
                left[k][...] = total.astype(bf16)

    return kernel


def scatter(parts, paths, place, name):
    ins = []
    for path, group in zip(paths, chunked(parts, RING)):
        ins += [group[0]] + [sent(group[k], path[0], k) for k in range(1, RING)]
    ff = parts[0].shape[2]
    shapes = [sds((hi - lo, ff), bf16) for _, _, lo, hi in paths for _ in range(RING)]
    mid = pl.pallas_call(
        sum_kernel(paths), out_shape=shapes, in_specs=[SM] + [VB] * len(ins), compiler_params=PARAMS, name=name
    )(place, *ins)
    arrived = []
    for path, group in zip(paths, chunked(mid, RING)):
        arrived += [group[0]] + [sent(group[k], path[1], k) for k in range(1, RING)]
    return arrived


def final_kernel(paths, scale, with_sigma):
    def kernel(*refs):
        ls = refs[0] if with_sigma else None
        ins, out = refs[int(with_sigma) : -1], refs[-1]
        for n in range(out.shape[0]):
            at = slice(n * LANE, (n + 1) * LANE)
            for (_, _, lo, hi), group in zip(paths, chunked(ins, RING)):
                total = group[0][:, at].astype(f32)
                for r in group[1:]:
                    total = total + r[:, at].astype(f32)
                if with_sigma:
                    total = total * jnp.exp(ls[n, lo:hi])
                out[n, lo:hi] = total * scale

    return kernel


def final(arrived, paths, shape, scale, ls, name):
    args = ([] if ls is None else [ls]) + list(arrived)
    return pl.pallas_call(
        final_kernel(paths, scale, ls is not None), out_shape=sds(shape, f32), compiler_params=PARAMS, name=name
    )(*args)


def early_kernel(rows, place, tok, cot, *refs):
    outs, (sq_out, sqt_out, tokt, held, sq, sqt, sems) = refs[:-7], refs[-7:]
    blocks = tok.shape[1] // LANE
    ks = rows.shape[1]
    for k in range(blocks):
        at = slice(k * LANE, (k + 1) * LANE)
        wide = tok[:, at].astype(f32)
        sq[:, at] = (wide * wide).astype(bf16)
        turned = tok[:, at].T
        tokt[k] = turned
        wide = turned.astype(f32)
        sqt[k] = (wide * wide).astype(bf16)
    saves = [pltpu.make_async_copy(sq, sq_out, sems.at[0]), pltpu.make_async_copy(sqt, sqt_out, sems.at[1])]
    for c in saves:
        c.start()

    def step(n, _):
        lhs = jnp.concatenate([tokt[rows[n, s]] for s in range(ks)], axis=0)
        part = jnp.dot(lhs, cot[:, at_block(n)], preferred_element_type=f32)
        held[:, :, :, at_block(n)] = part.astype(bf16).reshape(RING, RING, -1, LANE)
        return 0

    lax.fori_loop(0, cot.shape[1] // LANE, step, 0)
    copies = scatter_copies(place, SCATTER_THETA, held, chunked(outs, RING), sems.at[2])
    for c in copies:
        c.start()
    for c in saves + copies:
        c.wait()


def early(rows, place, tok, cot, own):
    t, d = tok.shape
    ff = cot.shape[1]
    shapes = scatter_shapes(SCATTER_THETA, ff) + [sds((t, d), bf16), sds((d // LANE, LANE, t), bf16)]
    outs = pl.pallas_call(
        early_kernel,
        out_shape=shapes,
        in_specs=[SM, SM, VB, VB],
        out_specs=[HB] * len(shapes),
        scratch_shapes=[
            pltpu.VMEM((d // LANE, LANE, t), bf16),
            pltpu.VMEM((RING, RING, own, ff), bf16),
            pltpu.VMEM((t, d), bf16),
            pltpu.VMEM((d // LANE, LANE, t), bf16),
            pltpu.SemaphoreType.DMA((3,)),
        ],
        compiler_params=PARAMS,
        name="early",
    )(rows, place, tok, cot)
    return outs[:-2], outs[-2], outs[-1]


def middle_kernel(rows, place, sq_in, sqt_in, noise, cot, *refs):
    n_in = RING * len(GATHER_SIGMA)
    sigma_refs, outs = refs[:n_in], refs[n_in:-9]
    gv_out, rn_out, sq, sqt, whole, held, gv, rn, sems = refs[-9:]
    ks = rows.shape[1]
    loads = gather_copies(place, GATHER_SIGMA, chunked(sigma_refs, RING), whole, sems.at[0])
    loads.append(pltpu.make_async_copy(sq_in, sq, sems.at[1]))
    late = pltpu.make_async_copy(sqt_in, sqt, sems.at[2])
    for c in loads:
        c.start()
    late.start()
    for c in loads:
        c.wait()

    def step(n, _):
        at = at_block(n)
        lhs = jnp.concatenate([sq[:, at_block(rows[n, s])] for s in range(ks)], axis=1)
        var = jnp.dot(lhs, block_column(whole, n), preferred_element_type=f32)
        root = jnp.sqrt(var + EPS)
        draw = noise[:, at].astype(f32)
        rn[:, at] = root * draw
        grad = (cot[:, at].astype(f32) * draw / (2.0 * root)).astype(bf16)
        gv[:, at] = grad

        @pl.when(n == 0)
        def _():
            late.wait()

        lhs = jnp.concatenate([sqt[rows[n, s]] for s in range(ks)], axis=0)
        part = jnp.dot(lhs, grad, preferred_element_type=f32)
        held[:, :, :, at] = part.astype(bf16).reshape(RING, RING, -1, LANE)
        return 0

    lax.fori_loop(0, cot.shape[1] // LANE, step, 0)
    copies = scatter_copies(place, SCATTER_VAR, held, chunked(outs, RING), sems.at[3])
    copies.append(pltpu.make_async_copy(gv, gv_out, sems.at[4]))
    copies.append(pltpu.make_async_copy(rn, rn_out, sems.at[5]))
    for c in copies:
        c.start()
    for c in copies:
        c.wait()


def middle(rows, place, sq, sqt, noise, cot, sigma, own):
    t, d = sq.shape
    ff = cot.shape[1]
    shapes = scatter_shapes(SCATTER_VAR, ff) + [sds((t, ff), bf16), sds((t, ff), f32)]
    refs = [r for group in sigma for r in group]
    outs = pl.pallas_call(
        middle_kernel,
        out_shape=shapes,
        in_specs=[SM, SM, HB, HB, VB, VB] + [HB] * len(refs),
        out_specs=[HB] * len(shapes),
        scratch_shapes=[
            pltpu.VMEM((t, d), bf16),
            pltpu.VMEM((d // LANE, LANE, t), bf16),
            pltpu.VMEM((RING, RING, own, ff), bf16),
            pltpu.VMEM((RING, RING, own, ff), bf16),
            pltpu.VMEM((t, ff), bf16),
            pltpu.VMEM((t, ff), f32),
            pltpu.SemaphoreType.DMA((6,)),
        ],
        compiler_params=PARAMS,
        name="middle",
    )(rows, place, sq, sqt, noise, cot, *refs)
    return outs[:-2], outs[-2], outs[-1]


def late_kernel(rows, place, tok, cot, gv, rn, *refs):
    n_s, n_t = RING * len(GATHER_SIGMA), RING * len(GATHER_THETA)
    sigma_refs, theta_refs = refs[:n_s], refs[n_s : n_s + n_t]
    out, away, home, sigma, theta, acc, sem = refs[n_s + n_t :]
    ks = rows.shape[1]
    loads = gather_copies(place, GATHER_SIGMA, chunked(sigma_refs, RING), sigma, sem)
    loads += gather_copies(place, GATHER_THETA, chunked(theta_refs, RING), theta, sem)
    for c in loads:
        c.start()
    acc[...] = jnp.zeros_like(acc)
    for c in loads:
        c.wait()

    def step(n, _):
        at = at_block(n)
        th = block_column(theta, n)
        sg = block_column(sigma, n)
        lhs = jnp.concatenate([tok[:, at_block(rows[n, s])] for s in range(ks)], axis=1)
        mean = jnp.dot(lhs, th, preferred_element_type=f32)
        out[:, at] = (mean + rn[:, at]).astype(bf16)
        first = lax.dot_general(cot[:, at], th, NT, preferred_element_type=f32)
        second = lax.dot_general(gv[:, at], sg, NT, preferred_element_type=f32)
        for s in range(ks):
            pick = at_block(rows[n, s])
            p = slice(s * LANE, (s + 1) * LANE)
            acc[:, pick] += first[:, p] + 2.0 * tok[:, pick].astype(f32) * second[:, p]
        return 0

    lax.fori_loop(0, cot.shape[1] // LANE, step, 0)
    w = away.shape[2]
    core = place[PLACE["core"]]
    for k in range(RING):
        y = (place[PLACE["y"]] + k) & 3
        home[k] = acc[:, pl.ds(pl.multiple_of((y * 2 + core) * w, w), w)].astype(bf16)
        away[k] = acc[:, pl.ds(pl.multiple_of((y * 2 + 1 - core) * w, w), w)].astype(bf16)


def late(rows, place, tok, cot, gv, rn, sigma, theta, own):
    t, d = tok.shape
    ff = cot.shape[1]
    w = d // (2 * RING)
    refs = [r for group in sigma + theta for r in group]
    return pl.pallas_call(
        late_kernel,
        out_shape=[sds((t, ff), bf16), sds((RING, t, w), bf16), sds((RING, t, w), bf16)],
        in_specs=[SM, SM] + [VB] * 4 + [HB] * len(refs),
        out_specs=[VB] * 3,
        scratch_shapes=[
            pltpu.VMEM((RING, RING, own, ff), bf16),
            pltpu.VMEM((RING, RING, own, ff), bf16),
            pltpu.VMEM((t, d), f32),
            pltpu.SemaphoreType.DMA(()),
        ],
        compiler_params=PARAMS,
        name="late",
    )(rows, place, tok, cot, gv, rn, *refs)


def pair_kernel(home, came, *outs):
    for k in range(RING):
        outs[k][...] = (home[k].astype(f32) + came[k].astype(f32)).astype(bf16)


def body(tokens, theta, log_sigma2, block_rows, noise, cotangent):
    place = jnp.stack([lax.axis_index(a) for a in ROW + COL]).astype(jnp.int32)
    own = theta.shape[1]
    sg, th = prep(log_sigma2, theta)
    sigma_in = gather(sg, GATHER_SIGMA)
    theta_in = gather(th, GATHER_THETA)
    parts_theta, sq, sqt = early(block_rows, place, tokens, cotangent, own)
    parts_var, gv, rn = middle(block_rows, place, sq, sqt, noise, cotangent, sigma_in, own)
    output, away, home = late(block_rows, place, tokens, cotangent, gv, rn, sigma_in, theta_in, own)
    tokens_all = tokens.shape[0] * lax.axis_size(ROW)
    width = block_rows.shape[1] * LANE
    inv_root = 1.0 / math.sqrt(tokens_all)
    got_theta = scatter(parts_theta, SCATTER_THETA, place, "sum_theta")
    grad_theta = final(got_theta, SCATTER_THETA, theta.shape, inv_root, None, "final_theta")
    got_var = scatter(parts_var, SCATTER_VAR, place, "sum_var")
    grad_logvar = final(got_var, SCATTER_VAR, theta.shape, width * inv_root, log_sigma2, "final_var")
    came = sent(away, "core", 1)
    t, w = home.shape[1:]
    pairs = pl.pallas_call(pair_kernel, out_shape=[sds((t, w), bf16)] * RING, compiler_params=PARAMS, name="pair")(
        home, came
    )
    grad_tokens = pairs[0].astype(f32)
    for k in range(1, RING):
        grad_tokens = grad_tokens + sent(pairs[k], "y", k).astype(f32)
    return (output, grad_tokens, grad_theta, grad_logvar)


def solution(mesh):
    finer = Mesh(mesh.devices.reshape(4, 4, 4, 2), ROW + COL)
    in_specs = (P(ROW, None), P(COL, ROW, None), P(COL, ROW, None), P(COL, None), P(ROW, COL), P(ROW, COL))
    out_specs = (P(ROW, COL), P(ROW, COL), P(COL, ROW, None), P(COL, ROW, None))
    return jax.shard_map(body, mesh=finer, in_specs=in_specs, out_specs=out_specs, check_vma=False)
```

```python
import math

import jax
import jax.numpy as jnp
from jax import lax
from jax.experimental import pallas as pl
from jax.experimental.pallas import tpu as pltpu
from jax.sharding import Mesh
from jax.sharding import PartitionSpec as P


ROW = ("z", "x")
COL = ("y", "core")
RING = 4
EPS = 1e-06
LANE = 128
f32, bf16 = jnp.float32, jnp.bfloat16
PARAMS = pltpu.CompilerParams(vmem_limit_bytes=60 * 1024 * 1024)
SM = pl.BlockSpec(memory_space=pltpu.SMEM)
VB = pl.BlockSpec(memory_space=pltpu.VMEM)
HB = pl.BlockSpec(memory_space=pl.ANY)
NT = (((1,), (1,)), ((), ()))

GATHER_SIGMA = (("x", "z", 0, 64),)
GATHER_THETA = (("z", "x", 0, 64),)
SCATTER_THETA = (("x", "z", 0, 64),)
SCATTER_VAR = (("z", "x", 0, 64),)
PLACE = {"z": 0, "x": 1, "y": 2, "core": 3}


def sds(shape, dtype):
    return jax.ShapeDtypeStruct(shape, dtype)


def at_block(index):
    return pl.ds(pl.multiple_of(index * LANE, LANE), LANE)


def sent(value, axis, step):
    n = lax.axis_size(axis)
    return lax.ppermute(value, axis, [(i, (i + step) % n) for i in range(n)])


def steps_of(value, axis):
    return [sent(value, axis, k) for k in range(1, RING)]


def steps_sent(values, axis):
    return [values[0]] + [sent(values[k], axis, k) for k in range(1, RING)]


def prep_kernel(paths_s, paths_t):
    def kernel(ls_ref, theta_ref, *outs):
        for n in range(theta_ref.shape[0]):
            at = slice(n * LANE, (n + 1) * LANE)
            for (_, _, lo, hi), o in zip(paths_s, outs):
                o[:, at] = jnp.exp(ls_ref[n, lo:hi]).astype(bf16)
            for (_, _, lo, hi), o in zip(paths_t, outs[len(paths_s) :]):
                o[:, at] = theta_ref[n, lo:hi]

    return kernel


def prep(ls, theta):
    c, _, b = theta.shape
    shapes = [sds((hi - lo, c * b), bf16) for _, _, lo, hi in GATHER_SIGMA + GATHER_THETA]
    outs = pl.pallas_call(
        prep_kernel(GATHER_SIGMA, GATHER_THETA), out_shape=shapes, compiler_params=PARAMS, name="prep"
    )(ls, theta)
    return outs[: len(GATHER_SIGMA)], outs[len(GATHER_SIGMA) :]


def gather(pieces, paths):
    blocks = [jnp.stack([p] + steps_of(p, path[0])) for p, path in zip(pieces, paths)]
    return [[b] + steps_of(b, path[1]) for b, path in zip(blocks, paths)]


def gather_copies(place, paths, groups, whole, sem):
    copies = []
    for (one, two, lo, hi), refs in zip(paths, groups):
        for k in range(RING):
            for j in range(RING):
                spot = {one: (place[PLACE[one]] - j) & 3, two: (place[PLACE[two]] - k) & 3}
                copies.append(pltpu.make_async_copy(refs[k].at[j], whole.at[spot["z"], spot["x"], lo:hi, :], sem))
    return copies


def chunked(refs, size):
    return [refs[i : i + size] for i in range(0, len(refs), size)]


def block_column(whole, n):
    blk = whole[:, :, :, at_block(n)]
    return blk.reshape(-1, LANE)


def scatter_copies(place, paths, held, groups, sem):
    copies = []
    for (one, _, lo, hi), refs in zip(paths, groups):
        for k in range(RING):
            spot = (place[PLACE[one]] + k) & 3
            src = held.at[spot, :, lo:hi, :] if one == "z" else held.at[:, spot, lo:hi, :]
            copies.append(pltpu.make_async_copy(src, refs[k], sem))
    return copies


def scatter_shapes(paths, ff):
    return [sds((RING, hi - lo, ff), bf16) for _, _, lo, hi in paths for _ in range(RING)]


def sum_kernel(paths):
    def kernel(place, *refs):
        ins, outs = refs[: RING * len(paths)], refs[RING * len(paths) :]
        for path, arrived, left in zip(paths, chunked(ins, RING), chunked(outs, RING)):
            own = place[PLACE[path[1]]]
            for k in range(RING):
                spot = (own + k) & 3
                total = arrived[0][spot].astype(f32)
                for r in arrived[1:]:
                    total = total + r[spot].astype(f32)
                left[k][...] = total.astype(bf16)

    return kernel


def scatter(parts, paths, place):
    ins = []
    for path, group in zip(paths, chunked(parts, RING)):
        ins += [group[0]] + [sent(group[k], path[0], k) for k in range(1, RING)]
    ff = parts[0].shape[2]
    shapes = [sds((hi - lo, ff), bf16) for _, _, lo, hi in paths for _ in range(RING)]
    mid = pl.pallas_call(
        sum_kernel(paths), out_shape=shapes, in_specs=[SM] + [VB] * len(ins), compiler_params=PARAMS
    )(place, *ins)
    arrived = []
    for path, group in zip(paths, chunked(mid, RING)):
        arrived += [group[0]] + [sent(group[k], path[1], k) for k in range(1, RING)]
    return arrived


def final_kernel(paths, scale, with_sigma):
    def kernel(*refs):
        ls = refs[0] if with_sigma else None
        ins, out = refs[int(with_sigma) : -1], refs[-1]
        for n in range(out.shape[0]):
            at = slice(n * LANE, (n + 1) * LANE)
            for (_, _, lo, hi), group in zip(paths, chunked(ins, RING)):
                total = group[0][:, at].astype(f32)
                for r in group[1:]:
                    total = total + r[:, at].astype(f32)
                if with_sigma:
                    total = total * jnp.exp(ls[n, lo:hi])
                out[n, lo:hi] = total * scale

    return kernel


def final(arrived, paths, shape, scale, ls):
    args = ([] if ls is None else [ls]) + list(arrived)
    return pl.pallas_call(
        final_kernel(paths, scale, ls is not None), out_shape=sds(shape, f32), compiler_params=PARAMS
    )(*args)


def early_kernel(rows, place, tok, cot, *refs):
    outs, (sq_out, sqt_out, tokt, held, sq, sqt, sems) = refs[:-7], refs[-7:]
    blocks = tok.shape[1] // LANE
    ks = rows.shape[1]
    for k in range(blocks):
        at = slice(k * LANE, (k + 1) * LANE)
        wide = tok[:, at].astype(f32)
        sq[:, at] = (wide * wide).astype(bf16)
        turned = tok[:, at].T
        tokt[k] = turned
        wide = turned.astype(f32)
        sqt[k] = (wide * wide).astype(bf16)
    saves = [pltpu.make_async_copy(sq, sq_out, sems.at[0]), pltpu.make_async_copy(sqt, sqt_out, sems.at[1])]
    for c in saves:
        c.start()

    def step(n, _):
        lhs = jnp.concatenate([tokt[rows[n, s]] for s in range(ks)], axis=0)
        part = jnp.dot(lhs, cot[:, at_block(n)], preferred_element_type=f32)
        held[:, :, :, at_block(n)] = part.astype(bf16).reshape(RING, RING, -1, LANE)
        return 0

    lax.fori_loop(0, cot.shape[1] // LANE, step, 0)
    copies = scatter_copies(place, SCATTER_THETA, held, chunked(outs, RING), sems.at[2])
    for c in copies:
        c.start()
    for c in saves + copies:
        c.wait()


def early(rows, place, tok, cot, own):
    t, d = tok.shape
    ff = cot.shape[1]
    shapes = scatter_shapes(SCATTER_THETA, ff) + [sds((t, d), bf16), sds((d // LANE, LANE, t), bf16)]
    outs = pl.pallas_call(
        early_kernel,
        out_shape=shapes,
        in_specs=[SM, SM, VB, VB],
        out_specs=[HB] * len(shapes),
        scratch_shapes=[
            pltpu.VMEM((d // LANE, LANE, t), bf16),
            pltpu.VMEM((RING, RING, own, ff), bf16),
            pltpu.VMEM((t, d), bf16),
            pltpu.VMEM((d // LANE, LANE, t), bf16),
            pltpu.SemaphoreType.DMA((3,)),
        ],
        compiler_params=PARAMS,
        name="early",
    )(rows, place, tok, cot)
    return outs[:-2], outs[-2], outs[-1]


def middle_kernel(rows, place, sq_in, sqt_in, noise, cot, *refs):
    n_in = RING * len(GATHER_SIGMA)
    sigma_refs, outs = refs[:n_in], refs[n_in:-9]
    gv_out, rn_out, sq, sqt, whole, held, gv, rn, sems = refs[-9:]
    ks = rows.shape[1]
    loads = gather_copies(place, GATHER_SIGMA, chunked(sigma_refs, RING), whole, sems.at[0])
    loads.append(pltpu.make_async_copy(sq_in, sq, sems.at[1]))
    late = pltpu.make_async_copy(sqt_in, sqt, sems.at[2])
    for c in loads:
        c.start()
    late.start()
    for c in loads:
        c.wait()

    def step(n, _):
        at = at_block(n)
        lhs = jnp.concatenate([sq[:, at_block(rows[n, s])] for s in range(ks)], axis=1)
        var = jnp.dot(lhs, block_column(whole, n), preferred_element_type=f32)
        root = jnp.sqrt(var + EPS)
        draw = noise[:, at].astype(f32)
        rn[:, at] = root * draw
        grad = (cot[:, at].astype(f32) * draw / (2.0 * root)).astype(bf16)
        gv[:, at] = grad

        @pl.when(n == 0)
        def _():
            late.wait()

        lhs = jnp.concatenate([sqt[rows[n, s]] for s in range(ks)], axis=0)
        part = jnp.dot(lhs, grad, preferred_element_type=f32)
        held[:, :, :, at] = part.astype(bf16).reshape(RING, RING, -1, LANE)
        return 0

    lax.fori_loop(0, cot.shape[1] // LANE, step, 0)
    copies = scatter_copies(place, SCATTER_VAR, held, chunked(outs, RING), sems.at[3])
    copies.append(pltpu.make_async_copy(gv, gv_out, sems.at[4]))
    copies.append(pltpu.make_async_copy(rn, rn_out, sems.at[5]))
    for c in copies:
        c.start()
    for c in copies:
        c.wait()


def middle(rows, place, sq, sqt, noise, cot, sigma, own):
    t, d = sq.shape
    ff = cot.shape[1]
    shapes = scatter_shapes(SCATTER_VAR, ff) + [sds((t, ff), bf16), sds((t, ff), f32)]
    refs = [r for group in sigma for r in group]
    outs = pl.pallas_call(
        middle_kernel,
        out_shape=shapes,
        in_specs=[SM, SM, HB, HB, VB, VB] + [HB] * len(refs),
        out_specs=[HB] * len(shapes),
        scratch_shapes=[
            pltpu.VMEM((t, d), bf16),
            pltpu.VMEM((d // LANE, LANE, t), bf16),
            pltpu.VMEM((RING, RING, own, ff), bf16),
            pltpu.VMEM((RING, RING, own, ff), bf16),
            pltpu.VMEM((t, ff), bf16),
            pltpu.VMEM((t, ff), f32),
            pltpu.SemaphoreType.DMA((6,)),
        ],
        compiler_params=PARAMS,
        name="middle",
    )(rows, place, sq, sqt, noise, cot, *refs)
    return outs[:-2], outs[-2], outs[-1]


def late_kernel(rows, place, tok, cot, gv, rn, *refs):
    n_s, n_t = RING * len(GATHER_SIGMA), RING * len(GATHER_THETA)
    sigma_refs, theta_refs = refs[:n_s], refs[n_s : n_s + n_t]
    out, away, home, sigma, theta, acc, sem = refs[n_s + n_t :]
    ks = rows.shape[1]
    loads = gather_copies(place, GATHER_SIGMA, chunked(sigma_refs, RING), sigma, sem)
    loads += gather_copies(place, GATHER_THETA, chunked(theta_refs, RING), theta, sem)
    for c in loads:
        c.start()
    acc[...] = jnp.zeros_like(acc)
    for c in loads:
        c.wait()

    def step(n, _):
        at = at_block(n)
        th = block_column(theta, n)
        sg = block_column(sigma, n)
        lhs = jnp.concatenate([tok[:, at_block(rows[n, s])] for s in range(ks)], axis=1)
        mean = jnp.dot(lhs, th, preferred_element_type=f32)
        out[:, at] = (mean + rn[:, at]).astype(bf16)
        first = lax.dot_general(cot[:, at], th, NT, preferred_element_type=f32)
        second = lax.dot_general(gv[:, at], sg, NT, preferred_element_type=f32)
        for s in range(ks):
            pick = at_block(rows[n, s])
            p = slice(s * LANE, (s + 1) * LANE)
            acc[:, pick] += first[:, p] + 2.0 * tok[:, pick].astype(f32) * second[:, p]
        return 0

    lax.fori_loop(0, cot.shape[1] // LANE, step, 0)
    w = away.shape[2]
    core = place[PLACE["core"]]
    for k in range(RING):
        y = (place[PLACE["y"]] + k) & 3
        home[k] = acc[:, pl.ds(pl.multiple_of((y * 2 + core) * w, w), w)].astype(bf16)
        away[k] = acc[:, pl.ds(pl.multiple_of((y * 2 + 1 - core) * w, w), w)].astype(bf16)


def late(rows, place, tok, cot, gv, rn, sigma, theta, own):
    t, d = tok.shape
    ff = cot.shape[1]
    w = d // (2 * RING)
    refs = [r for group in sigma + theta for r in group]
    return pl.pallas_call(
        late_kernel,
        out_shape=[sds((t, ff), bf16), sds((RING, t, w), bf16), sds((RING, t, w), bf16)],
        in_specs=[SM, SM] + [VB] * 4 + [HB] * len(refs),
        out_specs=[VB] * 3,
        scratch_shapes=[
            pltpu.VMEM((RING, RING, own, ff), bf16),
            pltpu.VMEM((RING, RING, own, ff), bf16),
            pltpu.VMEM((t, d), f32),
            pltpu.SemaphoreType.DMA(()),
        ],
        compiler_params=PARAMS,
        name="late",
    )(rows, place, tok, cot, gv, rn, *refs)


def pair_kernel(home, came, *outs):
    for k in range(RING):
        outs[k][...] = (home[k].astype(f32) + came[k].astype(f32)).astype(bf16)


def step(tokens, theta, log_sigma2, block_rows, noise, cotangent):
    place = jnp.stack([lax.axis_index(a) for a in ROW + COL]).astype(jnp.int32)
    own = theta.shape[1]
    sg, th = prep(log_sigma2, theta)
    sigma_in = gather(sg, GATHER_SIGMA)
    theta_in = gather(th, GATHER_THETA)
    parts_theta, sq, sqt = early(block_rows, place, tokens, cotangent, own)
    parts_var, gv, rn = middle(block_rows, place, sq, sqt, noise, cotangent, sigma_in, own)
    output, away, home = late(block_rows, place, tokens, cotangent, gv, rn, sigma_in, theta_in, own)
    tokens_all = tokens.shape[0] * lax.axis_size(ROW)
    width = block_rows.shape[1] * LANE
    inv_root = 1.0 / math.sqrt(tokens_all)
    got_theta = scatter(parts_theta, SCATTER_THETA, place)
    grad_theta = final(got_theta, SCATTER_THETA, theta.shape, inv_root, None)
    got_var = scatter(parts_var, SCATTER_VAR, place)
    grad_logvar = final(got_var, SCATTER_VAR, theta.shape, width * inv_root, log_sigma2)
    came = sent(away, "core", 1)
    t, w = home.shape[1:]
    pairs = pl.pallas_call(pair_kernel, out_shape=[sds((t, w), bf16)] * RING, compiler_params=PARAMS, name="pair")(
        home, came
    )
    arrived = steps_sent(pairs, "y")
    grad_tokens = arrived[0].astype(f32)
    for a in arrived[1:]:
        grad_tokens = grad_tokens + a.astype(f32)
    return (output, grad_tokens, grad_theta, grad_logvar)


def solution(mesh):
    finer = Mesh(mesh.devices.reshape(4, 4, 4, 2), ROW + COL)
    in_specs = (P(ROW, None), P(COL, ROW, None), P(COL, ROW, None), P(COL, None), P(ROW, COL), P(ROW, COL))
    out_specs = (P(ROW, COL), P(ROW, COL), P(COL, ROW, None), P(COL, ROW, None))
    return jax.shard_map(step, mesh=finer, in_specs=in_specs, out_specs=out_specs, check_vma=False)
```

```python
import math

import jax
import jax.numpy as jnp
from jax import lax
from jax.experimental import pallas as pl
from jax.experimental.pallas import tpu as pltpu
from jax.sharding import Mesh
from jax.sharding import PartitionSpec as P


ROW = ("z", "x")
COL = ("y", "core")
RING = 4
EPS = 1e-06
LANE = 128
f32, bf16 = jnp.float32, jnp.bfloat16
PARAMS = pltpu.CompilerParams(vmem_limit_bytes=60 * 1024 * 1024)
SM = pl.BlockSpec(memory_space=pltpu.SMEM)
VB = pl.BlockSpec(memory_space=pltpu.VMEM)
HB = pl.BlockSpec(memory_space=pl.ANY)
NT = (((1,), (1,)), ((), ()))

GATHER_SIGMA = (("x", "z", 0, 64),)
GATHER_THETA = (("z", "x", 0, 64),)
SCATTER_THETA = (("x", "z", 0, 64),)
SCATTER_VAR = (("z", "x", 0, 64),)
PLACE = {"z": 0, "x": 1, "y": 2, "core": 3}


def sds(shape, dtype):
    return jax.ShapeDtypeStruct(shape, dtype)


def at_block(index):
    return pl.ds(pl.multiple_of(index * LANE, LANE), LANE)


def sent(value, axis, step):
    n = lax.axis_size(axis)
    return lax.ppermute(value, axis, [(i, (i + step) % n) for i in range(n)])


def steps_of(value, axis):
    return [sent(value, axis, k) for k in range(1, RING)]


def steps_sent(values, axis):
    return [values[0]] + [sent(values[k], axis, k) for k in range(1, RING)]


def prep_kernel(paths_s, paths_t):
    def kernel(ls_ref, theta_ref, *outs):
        for n in range(theta_ref.shape[0]):
            at = slice(n * LANE, (n + 1) * LANE)
            for (_, _, lo, hi), o in zip(paths_s, outs):
                o[:, at] = jnp.exp(ls_ref[n, lo:hi]).astype(bf16)
            for (_, _, lo, hi), o in zip(paths_t, outs[len(paths_s) :]):
                o[:, at] = theta_ref[n, lo:hi]

    return kernel


def prep(ls, theta):
    c, _, b = theta.shape
    shapes = [sds((hi - lo, c * b), bf16) for _, _, lo, hi in GATHER_SIGMA + GATHER_THETA]
    outs = pl.pallas_call(
        prep_kernel(GATHER_SIGMA, GATHER_THETA), out_shape=shapes, compiler_params=PARAMS, name="prep"
    )(ls, theta)
    return outs[: len(GATHER_SIGMA)], outs[len(GATHER_SIGMA) :]


def gather(pieces, paths):
    blocks = [jnp.stack([p] + steps_of(p, path[0])) for p, path in zip(pieces, paths)]
    return [[b] + steps_of(b, path[1]) for b, path in zip(blocks, paths)]


def chunked(refs, size):
    return [refs[i : i + size] for i in range(0, len(refs), size)]


def block_column(whole, n):
    blk = whole[:, :, :, at_block(n)]
    return blk.reshape(-1, LANE)


def scatter_shapes(paths, ff):
    return [sds((RING, hi - lo, ff), bf16) for _, _, lo, hi in paths for _ in range(RING)]


def summed(arrived, spot):
    total = arrived[0][spot].astype(f32)
    for r in arrived[1:]:
        total = total + r[spot].astype(f32)
    return total.astype(bf16)


def scatter(parts, paths):
    ins = []
    for path, group in zip(paths, chunked(parts, RING)):
        ins += [group[0]] + [sent(group[k], path[0], k) for k in range(1, RING)]
    mid = [summed(group, k) for group in chunked(ins, RING) for k in range(RING)]
    arrived = []
    for path, group in zip(paths, chunked(mid, RING)):
        arrived += [group[0]] + [sent(group[k], path[1], k) for k in range(1, RING)]
    return arrived


def final_kernel(paths, scale, with_sigma):
    def kernel(*refs):
        ls = refs[0] if with_sigma else None
        ins, out = refs[int(with_sigma) : -1], refs[-1]
        for n in range(out.shape[0]):
            at = slice(n * LANE, (n + 1) * LANE)
            for (_, _, lo, hi), group in zip(paths, chunked(ins, RING)):
                total = group[0][:, at].astype(f32)
                for r in group[1:]:
                    total = total + r[:, at].astype(f32)
                if with_sigma:
                    total = total * jnp.exp(ls[n, lo:hi])
                out[n, lo:hi] = total * scale

    return kernel


def final(arrived, paths, shape, scale, ls):
    args = ([] if ls is None else [ls]) + list(arrived)
    return pl.pallas_call(
        final_kernel(paths, scale, ls is not None), out_shape=sds(shape, f32), compiler_params=PARAMS
    )(*args)


GROUPS = 2


def issue(copies):
    for c in copies:
        c.start()


def column_span(group, per):
    w = per * LANE
    return pl.ds(pl.multiple_of(group * w, w), w)


def gather_starts(place, paths, groups, whole, sems, per):
    for g in range(GROUPS):
        cols = slice(g * per * LANE, (g + 1) * per * LANE)
        for (one, two, lo, hi), refs in zip(paths, groups):
            for k in range(RING):
                for j in range(RING):
                    spot = {one: (place[PLACE[one]] - j) & 3, two: (place[PLACE[two]] - k) & 3}
                    pltpu.make_async_copy(
                        refs[k].at[j, :, cols], whole.at[spot["z"], spot["x"], lo:hi, cols], sems.at[g]
                    ).start()


def gather_wait(whole, sems, g, per):
    cols = column_span(g, per)
    part = whole.at[:, :, :, cols]
    pltpu.make_async_copy(part, part, sems.at[g]).wait()


def scatter_start(place, paths, held, groups, sem, cols):
    for (one, two, lo, hi), refs in zip(paths, groups):
        for k in range(RING):
            for j in range(RING):
                spot = {one: (place[PLACE[one]] + k) & 3, two: (place[PLACE[two]] + j) & 3}
                pltpu.make_async_copy(
                    held.at[spot["z"], spot["x"], lo:hi, cols], refs[k].at[j, :, cols], sem
                ).start()


def early_kernel(rows, tok, cot, *refs):
    outs, (sq_out, sqt_out, tokt, held, sq, sqt, sems) = refs[:-7], refs[-7:]
    place = [lax.axis_index(a) for a in ROW + COL]
    blocks = tok.shape[1] // LANE
    ks = rows.shape[1]
    per = cot.shape[1] // LANE // GROUPS
    for k in range(blocks):
        at = slice(k * LANE, (k + 1) * LANE)
        wide = tok[:, at].astype(f32)
        sq[:, at] = (wide * wide).astype(bf16)
        turned = tok[:, at].T
        tokt[k] = turned
        wide = turned.astype(f32)
        sqt[k] = (wide * wide).astype(bf16)
    saves = [pltpu.make_async_copy(sq, sq_out, sems.at[0]), pltpu.make_async_copy(sqt, sqt_out, sems.at[1])]
    issue(saves)

    def group(g, _):
        for u in range(per):
            n = g * per + u
            lhs = jnp.concatenate([tokt[rows[n, s]] for s in range(ks)], axis=0)
            part = jnp.dot(lhs, cot[:, at_block(n)], preferred_element_type=f32)
            held[:, :, :, at_block(n)] = part.astype(bf16).reshape(RING, RING, -1, LANE)
        scatter_start(place, SCATTER_THETA, held, chunked(outs, RING), sems.at[2], column_span(g, per))
        return 0

    lax.fori_loop(0, GROUPS, group, 0)
    for c in saves:
        c.wait()
    pltpu.make_async_copy(held, held, sems.at[2]).wait()


def early(rows, tok, cot, own):
    t, d = tok.shape
    ff = cot.shape[1]
    shapes = scatter_shapes(SCATTER_THETA, ff) + [sds((t, d), bf16), sds((d // LANE, LANE, t), bf16)]
    outs = pl.pallas_call(
        early_kernel,
        out_shape=shapes,
        in_specs=[SM, VB, VB],
        out_specs=[HB] * len(shapes),
        scratch_shapes=[
            pltpu.VMEM((d // LANE, LANE, t), bf16),
            pltpu.VMEM((RING, RING, own, ff), bf16),
            pltpu.VMEM((t, d), bf16),
            pltpu.VMEM((d // LANE, LANE, t), bf16),
            pltpu.SemaphoreType.DMA((3,)),
        ],
        compiler_params=PARAMS,
        name="early",
    )(rows, tok, cot)
    return outs[:-2], outs[-2], outs[-1]


def middle_kernel(rows, sq_in, sqt_in, noise_in, cot_in, *refs):
    n_in = RING * len(GATHER_SIGMA)
    sigma_refs, outs = refs[:n_in], refs[n_in:-14]
    gv_out, rn_out, sq, sqt, noise, cot, whole, held, gv, rn, s_sig, s_in, s_one, s_out = refs[-14:]
    place = [lax.axis_index(a) for a in ROW + COL]
    ks = rows.shape[1]
    per = noise.shape[1] // LANE // GROUPS
    first = pltpu.make_async_copy(sq_in, sq, s_one.at[0])
    second = pltpu.make_async_copy(sqt_in, sqt, s_one.at[1])
    first.start()
    gather_starts(place, GATHER_SIGMA, chunked(sigma_refs, RING), whole, s_sig, per)

    def loads(g):
        at = column_span(g, per)
        return [
            pltpu.make_async_copy(noise_in.at[:, at], noise.at[:, at], s_in.at[0, g]),
            pltpu.make_async_copy(cot_in.at[:, at], cot.at[:, at], s_in.at[1, g]),
        ]

    def saves(g):
        at = column_span(g, per)
        return [
            pltpu.make_async_copy(gv.at[:, at], gv_out.at[:, at], s_out.at[0, g]),
            pltpu.make_async_copy(rn.at[:, at], rn_out.at[:, at], s_out.at[1, g]),
        ]

    issue(loads(0))
    second.start()
    for g in range(1, GROUPS):
        issue(loads(g))
    first.wait()

    def group(g, _):
        gather_wait(whole, s_sig, g, per)
        for c in loads(g):
            c.wait()
        for u in range(per):
            n = g * per + u
            at = at_block(n)
            lhs = jnp.concatenate([sq[:, at_block(rows[n, s])] for s in range(ks)], axis=1)
            var = jnp.dot(lhs, block_column(whole, n), preferred_element_type=f32) + EPS
            inv = lax.rsqrt(var)
            draw = noise[:, at].astype(f32)
            rn[:, at] = var * inv * draw
            gv[:, at] = (cot[:, at].astype(f32) * draw * (0.5 * inv)).astype(bf16)

        @pl.when(g == 0)
        def _():
            second.wait()

        for u in range(per):
            n = g * per + u
            at = at_block(n)
            lhs = jnp.concatenate([sqt[rows[n, s]] for s in range(ks)], axis=0)
            part = jnp.dot(lhs, gv[:, at], preferred_element_type=f32)
            held[:, :, :, at] = part.astype(bf16).reshape(RING, RING, -1, LANE)
        issue(saves(g))
        scatter_start(place, SCATTER_VAR, held, chunked(outs, RING), s_one.at[2], column_span(g, per))
        return 0

    lax.fori_loop(0, GROUPS, group, 0)
    for g in range(GROUPS):
        for c in saves(g):
            c.wait()
    pltpu.make_async_copy(held, held, s_one.at[2]).wait()


def middle(rows, sq, sqt, noise, cot, sigma, own):
    t, d = sq.shape
    ff = cot.shape[1]
    shapes = scatter_shapes(SCATTER_VAR, ff) + [sds((t, ff), bf16), sds((t, ff), f32)]
    refs = [r for group in sigma for r in group]
    outs = pl.pallas_call(
        middle_kernel,
        out_shape=shapes,
        in_specs=[SM, HB, HB, HB, HB] + [HB] * len(refs),
        out_specs=[HB] * len(shapes),
        scratch_shapes=[
            pltpu.VMEM((t, d), bf16),
            pltpu.VMEM((d // LANE, LANE, t), bf16),
            pltpu.VMEM((t, ff), bf16),
            pltpu.VMEM((t, ff), bf16),
            pltpu.VMEM((RING, RING, own, ff), bf16),
            pltpu.VMEM((RING, RING, own, ff), bf16),
            pltpu.VMEM((t, ff), bf16),
            pltpu.VMEM((t, ff), f32),
            pltpu.SemaphoreType.DMA((GROUPS,)),
            pltpu.SemaphoreType.DMA((2, GROUPS)),
            pltpu.SemaphoreType.DMA((3,)),
            pltpu.SemaphoreType.DMA((2, GROUPS)),
        ],
        compiler_params=PARAMS,
        name="middle",
    )(rows, sq, sqt, noise, cot, *refs)
    return outs[:-2], outs[-2], outs[-1]


def late_kernel(rows, tok_in, cot_in, gv_in, rn_in, *refs):
    n_s, n_t = RING * len(GATHER_SIGMA), RING * len(GATHER_THETA)
    sigma_refs, theta_refs = refs[:n_s], refs[n_s : n_s + n_t]
    (out_out, away_out, home_out, tok, cot, gv, rn, out, both, sigma, theta, acc, s_w, s_in, s_one, s_out) = refs[n_s + n_t :]
    place = [lax.axis_index(a) for a in ROW + COL]
    ks = rows.shape[1]
    per = cot.shape[1] // LANE // GROUPS
    first = pltpu.make_async_copy(tok_in, tok, s_one.at[0])
    first.start()

    def loads(g):
        at = column_span(g, per)
        pairs = ((cot_in, cot), (gv_in, gv), (rn_in, rn))
        return [pltpu.make_async_copy(a.at[:, at], b.at[:, at], s_in.at[i, g]) for i, (a, b) in enumerate(pairs)]

    def save(g):
        at = column_span(g, per)
        return pltpu.make_async_copy(out.at[:, at], out_out.at[:, at], s_out.at[g])

    issue(loads(0))
    gather_starts(place, GATHER_THETA, chunked(theta_refs, RING), theta, s_w.at[0], per)
    gather_starts(place, GATHER_SIGMA, chunked(sigma_refs, RING), sigma, s_w.at[1], per)
    for g in range(1, GROUPS):
        issue(loads(g))
    acc[...] = jnp.zeros_like(acc)
    first.wait()

    def group(g, _):
        gather_wait(theta, s_w.at[0], g, per)
        gather_wait(sigma, s_w.at[1], g, per)
        for c in loads(g):
            c.wait()
        for u in range(per):
            n = g * per + u
            at = at_block(n)
            th = block_column(theta, n)
            sg = block_column(sigma, n)
            lhs = jnp.concatenate([tok[:, at_block(rows[n, s])] for s in range(ks)], axis=1)
            mean = jnp.dot(lhs, th, preferred_element_type=f32)
            out[:, at] = (mean + rn[:, at]).astype(bf16)
            for q in range(ks // 2):
                span = slice(q * 2 * LANE, (q + 1) * 2 * LANE)
                one = lax.dot_general(cot[:, at], th[span], NT, preferred_element_type=f32)
                two = lax.dot_general(gv[:, at], sg[span], NT, preferred_element_type=f32)
                for h in range(2):
                    pick = at_block(rows[n, 2 * q + h])
                    p = slice(h * LANE, (h + 1) * LANE)
                    acc[:, pick] += one[:, p] + 2.0 * tok[:, pick].astype(f32) * two[:, p]
        save(g).start()
        return 0

    lax.fori_loop(0, GROUPS, group, 0)
    w = away_out.shape[2]
    core = place[PLACE["core"]]
    ends = []
    for side, (ref, half) in enumerate(((away_out, 1 - core), (home_out, core))):
        for k in range(RING):
            y = (place[PLACE["y"]] + k) & 3
            both[side, k] = acc[:, pl.ds(pl.multiple_of((y * 2 + half) * w, w), w)].astype(bf16)
            ends.append(pltpu.make_async_copy(both.at[side, k], ref.at[k], s_one.at[1 + side * RING + k]))
            ends[-1].start()
    for c in [save(g) for g in range(GROUPS)] + ends:
        c.wait()


def late(rows, tok, cot, gv, rn, sigma, theta, own):
    t, d = tok.shape
    ff = cot.shape[1]
    w = d // (2 * RING)
    refs = [r for group in sigma + theta for r in group]
    shapes = [sds((t, ff), bf16), sds((RING, t, w), bf16), sds((RING, t, w), bf16)]
    return pl.pallas_call(
        late_kernel,
        out_shape=shapes,
        in_specs=[SM] + [HB] * (4 + len(refs)),
        out_specs=[HB] * 3,
        scratch_shapes=[
            pltpu.VMEM((t, d), bf16),
            pltpu.VMEM((t, ff), bf16),
            pltpu.VMEM((t, ff), bf16),
            pltpu.VMEM((t, ff), f32),
            pltpu.VMEM((t, ff), bf16),
            pltpu.VMEM((2, RING, t, w), bf16),
            pltpu.VMEM((RING, RING, own, ff), bf16),
            pltpu.VMEM((RING, RING, own, ff), bf16),
            pltpu.VMEM((t, d), f32),
            pltpu.SemaphoreType.DMA((2, GROUPS)),
            pltpu.SemaphoreType.DMA((3, GROUPS)),
            pltpu.SemaphoreType.DMA((1 + 2 * RING,)),
            pltpu.SemaphoreType.DMA((GROUPS,)),
        ],
        compiler_params=PARAMS,
        name="late",
    )(rows, tok, cot, gv, rn, *refs)


def step(tokens, theta, log_sigma2, block_rows, noise, cotangent):
    own = theta.shape[1]
    sg, th = prep(log_sigma2, theta)
    sigma_in = gather(sg, GATHER_SIGMA)
    theta_in = gather(th, GATHER_THETA)
    parts_theta, sq, sqt = early(block_rows, tokens, cotangent, own)
    parts_var, gv, rn = middle(block_rows, sq, sqt, noise, cotangent, sigma_in, own)
    output, away, home = late(block_rows, tokens, cotangent, gv, rn, sigma_in, theta_in, own)
    tokens_all = tokens.shape[0] * lax.axis_size(ROW)
    width = block_rows.shape[1] * LANE
    inv_root = 1.0 / math.sqrt(tokens_all)
    got_theta = scatter(parts_theta, SCATTER_THETA)
    grad_theta = final(got_theta, SCATTER_THETA, theta.shape, inv_root, None)
    got_var = scatter(parts_var, SCATTER_VAR)
    grad_logvar = final(got_var, SCATTER_VAR, theta.shape, width * inv_root, log_sigma2)
    came = sent(away, "core", 1)
    pairs = [(home[k].astype(f32) + came[k].astype(f32)).astype(bf16) for k in range(RING)]
    arrived = steps_sent(pairs, "y")
    grad_tokens = arrived[0].astype(f32)
    for a in arrived[1:]:
        grad_tokens = grad_tokens + a.astype(f32)
    return (output, grad_tokens, grad_theta, grad_logvar)


def solution(mesh):
    finer = Mesh(mesh.devices.reshape(4, 4, 4, 2), ROW + COL)
    in_specs = (P(ROW, None), P(COL, ROW, None), P(COL, ROW, None), P(COL, None), P(ROW, COL), P(ROW, COL))
    out_specs = (P(ROW, COL), P(ROW, COL), P(COL, ROW, None), P(COL, ROW, None))
    return jax.shard_map(step, mesh=finer, in_specs=in_specs, out_specs=out_specs, check_vma=False)
```

```python
import math

import jax
import jax.numpy as jnp
from jax import lax
from jax.experimental import pallas as pl
from jax.experimental.pallas import tpu as pltpu
from jax.sharding import Mesh
from jax.sharding import PartitionSpec as P


ROW = ("z", "x")
COL = ("y", "core")
RING = 4
EPS = 1e-06
LANE = 128
f32, bf16 = jnp.float32, jnp.bfloat16
PARAMS = pltpu.CompilerParams(vmem_limit_bytes=60 * 1024 * 1024)
SM = pl.BlockSpec(memory_space=pltpu.SMEM)
VB = pl.BlockSpec(memory_space=pltpu.VMEM)
HB = pl.BlockSpec(memory_space=pl.ANY)
NT = (((1,), (1,)), ((), ()))

GATHER_SIGMA = (("x", "z", 0, 32), ("z", "x", 32, 64))
GATHER_THETA = (("z", "x", 0, 64),)
SCATTER_THETA = (("z", "x", 0, 64),)
SCATTER_VAR = (("x", "z", 0, 64),)
PLACE = {"z": 0, "x": 1, "y": 2, "core": 3}


def sds(shape, dtype):
    return jax.ShapeDtypeStruct(shape, dtype)


def at_block(index):
    return pl.ds(pl.multiple_of(index * LANE, LANE), LANE)


def sent(value, axis, step):
    return lax.ppermute(value, axis, [(i, i ^ step) for i in range(lax.axis_size(axis))])


def steps_of(value, axis):
    return [sent(value, axis, k) for k in range(1, RING)]


def steps_sent(values, axis):
    return [values[0]] + [sent(values[k], axis, k) for k in range(1, RING)]


def prep_kernel(paths_s, paths_t):
    def kernel(ls_ref, theta_ref, *outs):
        for n in range(theta_ref.shape[0]):
            at = slice(n * LANE, (n + 1) * LANE)
            for (_, _, lo, hi), o in zip(paths_s, outs):
                o[:, at] = jnp.exp(ls_ref[n, lo:hi]).astype(bf16)
            for (_, _, lo, hi), o in zip(paths_t, outs[len(paths_s) :]):
                o[:, at] = theta_ref[n, lo:hi]

    return kernel


def prep(ls, theta):
    c, _, b = theta.shape
    shapes = [sds((hi - lo, c * b), bf16) for _, _, lo, hi in GATHER_SIGMA + GATHER_THETA]
    outs = pl.pallas_call(
        prep_kernel(GATHER_SIGMA, GATHER_THETA), out_shape=shapes, compiler_params=PARAMS, name="prep"
    )(ls, theta)
    return outs[: len(GATHER_SIGMA)], outs[len(GATHER_SIGMA) :]


def gather(pieces, paths):
    blocks = [jnp.stack([p] + steps_of(p, path[0])) for p, path in zip(pieces, paths)]
    return [[b] + steps_of(b, path[1]) for b, path in zip(blocks, paths)]


def chunked(refs, size):
    return [refs[i : i + size] for i in range(0, len(refs), size)]


def block_column(whole, n):
    blk = whole[:, :, :, at_block(n)]
    return blk.reshape(-1, LANE)


def scatter_shapes(paths, ff):
    return [sds((RING, hi - lo, ff), bf16) for _, _, lo, hi in paths for _ in range(RING)]


def summed(arrived, spot):
    total = arrived[0][spot].astype(f32)
    for r in arrived[1:]:
        total = total + r[spot].astype(f32)
    return total.astype(bf16)


def scatter(parts, paths):
    ins = []
    for path, group in zip(paths, chunked(parts, RING)):
        ins += [group[0]] + [sent(group[k], path[0], k) for k in range(1, RING)]
    mid = [summed(group, k) for group in chunked(ins, RING) for k in range(RING)]
    arrived = []
    for path, group in zip(paths, chunked(mid, RING)):
        arrived += [group[0]] + [sent(group[k], path[1], k) for k in range(1, RING)]
    return arrived


def final_kernel(paths, scale, with_sigma):
    def kernel(*refs):
        ls = refs[0] if with_sigma else None
        ins, out = refs[int(with_sigma) : -1], refs[-1]
        for n in range(out.shape[0]):
            at = slice(n * LANE, (n + 1) * LANE)
            for (_, _, lo, hi), group in zip(paths, chunked(ins, RING)):
                total = group[0][:, at].astype(f32)
                for r in group[1:]:
                    total = total + r[:, at].astype(f32)
                if with_sigma:
                    total = total * jnp.exp(ls[n, lo:hi])
                out[n, lo:hi] = total * scale

    return kernel


def final(arrived, paths, shape, scale, ls):
    args = ([] if ls is None else [ls]) + list(arrived)
    return pl.pallas_call(
        final_kernel(paths, scale, ls is not None), out_shape=sds(shape, f32), compiler_params=PARAMS
    )(*args)


EARLY_GROUPS, MIDDLE_GROUPS, LATE_GROUPS = 4, 2, 4


def issue(copies):
    for c in copies:
        c.start()


def column_span(group, per):
    w = per * LANE
    return pl.ds(pl.multiple_of(group * w, w), w)


def gather_starts(place, paths, groups, whole, sems, per, count):
    for g in range(count):
        cols = slice(g * per * LANE, (g + 1) * per * LANE)
        for (one, two, lo, hi), refs in zip(paths, groups):
            for k in range(RING):
                for j in range(RING):
                    spot = {one: place[PLACE[one]] ^ j, two: place[PLACE[two]] ^ k}
                    pltpu.make_async_copy(
                        refs[k].at[j, :, cols], whole.at[spot["z"], spot["x"], lo:hi, cols], sems.at[g]
                    ).start()


def gather_wait(whole, sems, g, per):
    cols = column_span(g, per)
    part = whole.at[:, :, :, cols]
    pltpu.make_async_copy(part, part, sems.at[g]).wait()


def scatter_start(place, paths, held, groups, sem, cols):
    for (one, two, lo, hi), refs in zip(paths, groups):
        for k in range(RING):
            for j in range(RING):
                spot = {one: place[PLACE[one]] ^ k, two: place[PLACE[two]] ^ j}
                pltpu.make_async_copy(
                    held.at[spot["z"], spot["x"], lo:hi, cols], refs[k].at[j, :, cols], sem
                ).start()


def early_kernel(rows, tok, cot, *refs):
    outs, (sq_out, sqt_out, tokt, held, sq, sqt, sems) = refs[:-7], refs[-7:]
    place = [lax.axis_index(a) for a in ROW + COL]
    blocks = tok.shape[1] // LANE
    ks = rows.shape[1]
    per = cot.shape[1] // LANE // EARLY_GROUPS
    for k in range(blocks):
        at = slice(k * LANE, (k + 1) * LANE)
        wide = tok[:, at].astype(f32)
        sq[:, at] = (wide * wide).astype(bf16)
        turned = tok[:, at].T
        tokt[k] = turned
        wide = turned.astype(f32)
        sqt[k] = (wide * wide).astype(bf16)
    saves = [pltpu.make_async_copy(sq, sq_out, sems.at[0]), pltpu.make_async_copy(sqt, sqt_out, sems.at[1])]
    issue(saves)

    def group(g, _):
        for u in range(per):
            n = g * per + u
            lhs = jnp.concatenate([tokt[rows[n, s]] for s in range(ks)], axis=0)
            part = jnp.dot(lhs, cot[:, at_block(n)], preferred_element_type=f32)
            held[:, :, :, at_block(n)] = part.astype(bf16).reshape(RING, RING, -1, LANE)
        scatter_start(place, SCATTER_THETA, held, chunked(outs, RING), sems.at[2], column_span(g, per))
        return 0

    lax.fori_loop(0, EARLY_GROUPS, group, 0)
    for c in saves:
        c.wait()
    pltpu.make_async_copy(held, held, sems.at[2]).wait()


def early(rows, tok, cot, own):
    t, d = tok.shape
    ff = cot.shape[1]
    shapes = scatter_shapes(SCATTER_THETA, ff) + [sds((t, d), bf16), sds((d // LANE, LANE, t), bf16)]
    outs = pl.pallas_call(
        early_kernel,
        out_shape=shapes,
        in_specs=[SM, VB, VB],
        out_specs=[HB] * len(shapes),
        scratch_shapes=[
            pltpu.VMEM((d // LANE, LANE, t), bf16),
            pltpu.VMEM((RING, RING, own, ff), bf16),
            pltpu.VMEM((t, d), bf16),
            pltpu.VMEM((d // LANE, LANE, t), bf16),
            pltpu.SemaphoreType.DMA((3,)),
        ],
        compiler_params=PARAMS,
        name="early",
    )(rows, tok, cot)
    return outs[:-2], outs[-2], outs[-1]


def middle_kernel(rows, sq_in, sqt_in, noise_in, cot_in, *refs):
    n_in = RING * len(GATHER_SIGMA)
    sigma_refs, outs = refs[:n_in], refs[n_in:-14]
    gv_out, rn_out, sq, sqt, noise, cot, whole, held, gv, rn, s_sig, s_in, s_one, s_out = refs[-14:]
    place = [lax.axis_index(a) for a in ROW + COL]
    ks = rows.shape[1]
    per = noise.shape[1] // LANE // MIDDLE_GROUPS
    first = pltpu.make_async_copy(sq_in, sq, s_one.at[0])
    second = pltpu.make_async_copy(sqt_in, sqt, s_one.at[1])
    first.start()
    gather_starts(place, GATHER_SIGMA, chunked(sigma_refs, RING), whole, s_sig, per, MIDDLE_GROUPS)

    def loads(g):
        at = column_span(g, per)
        return [
            pltpu.make_async_copy(noise_in.at[:, at], noise.at[:, at], s_in.at[0, g]),
            pltpu.make_async_copy(cot_in.at[:, at], cot.at[:, at], s_in.at[1, g]),
        ]

    def saves(g):
        at = column_span(g, per)
        return [
            pltpu.make_async_copy(gv.at[:, at], gv_out.at[:, at], s_out.at[0, g]),
            pltpu.make_async_copy(rn.at[:, at], rn_out.at[:, at], s_out.at[1, g]),
        ]

    issue(loads(0))
    second.start()
    for g in range(1, MIDDLE_GROUPS):
        issue(loads(g))
    first.wait()

    def group(g, _):
        gather_wait(whole, s_sig, g, per)
        for c in loads(g):
            c.wait()
        for u in range(per):
            n = g * per + u
            at = at_block(n)
            lhs = jnp.concatenate([sq[:, at_block(rows[n, s])] for s in range(ks)], axis=1)
            var = jnp.dot(lhs, block_column(whole, n), preferred_element_type=f32) + EPS
            inv = lax.rsqrt(var)
            draw = noise[:, at].astype(f32)
            rn[:, at] = var * inv * draw
            gv[:, at] = (cot[:, at].astype(f32) * draw * inv).astype(bf16)

        @pl.when(g == 0)
        def _():
            second.wait()

        for u in range(per):
            n = g * per + u
            at = at_block(n)
            lhs = jnp.concatenate([sqt[rows[n, s]] for s in range(ks)], axis=0)
            part = jnp.dot(lhs, gv[:, at], preferred_element_type=f32)
            held[:, :, :, at] = part.astype(bf16).reshape(RING, RING, -1, LANE)
        issue(saves(g))
        scatter_start(place, SCATTER_VAR, held, chunked(outs, RING), s_one.at[2], column_span(g, per))
        return 0

    lax.fori_loop(0, MIDDLE_GROUPS, group, 0)
    for g in range(MIDDLE_GROUPS):
        for c in saves(g):
            c.wait()
    pltpu.make_async_copy(held, held, s_one.at[2]).wait()


def middle(rows, sq, sqt, noise, cot, sigma, own):
    t, d = sq.shape
    ff = cot.shape[1]
    shapes = scatter_shapes(SCATTER_VAR, ff) + [sds((t, ff), bf16), sds((t, ff), f32)]
    refs = [r for group in sigma for r in group]
    outs = pl.pallas_call(
        middle_kernel,
        out_shape=shapes,
        in_specs=[SM, HB, HB, HB, HB] + [HB] * len(refs),
        out_specs=[HB] * len(shapes),
        scratch_shapes=[
            pltpu.VMEM((t, d), bf16),
            pltpu.VMEM((d // LANE, LANE, t), bf16),
            pltpu.VMEM((t, ff), bf16),
            pltpu.VMEM((t, ff), bf16),
            pltpu.VMEM((RING, RING, own, ff), bf16),
            pltpu.VMEM((RING, RING, own, ff), bf16),
            pltpu.VMEM((t, ff), bf16),
            pltpu.VMEM((t, ff), f32),
            pltpu.SemaphoreType.DMA((MIDDLE_GROUPS,)),
            pltpu.SemaphoreType.DMA((2, MIDDLE_GROUPS)),
            pltpu.SemaphoreType.DMA((3,)),
            pltpu.SemaphoreType.DMA((2, MIDDLE_GROUPS)),
        ],
        compiler_params=PARAMS,
        name="middle",
    )(rows, sq, sqt, noise, cot, *refs)
    return outs[:-2], outs[-2], outs[-1]


def late_kernel(rows, tok_in, cot_in, gv_in, rn_in, *refs):
    n_s, n_t = RING * len(GATHER_SIGMA), RING * len(GATHER_THETA)
    sigma_refs, theta_refs = refs[:n_s], refs[n_s : n_s + n_t]
    (out_out, away_out, home_out, tok, cot, gv, rn, out, both, sigma, theta, acc, s_w, s_in, s_one, s_out) = refs[n_s + n_t :]
    place = [lax.axis_index(a) for a in ROW + COL]
    ks = rows.shape[1]
    per = cot.shape[1] // LANE // LATE_GROUPS
    first = pltpu.make_async_copy(tok_in, tok, s_one.at[0])
    first.start()

    def loads(g):
        at = column_span(g, per)
        pairs = ((cot_in, cot), (gv_in, gv), (rn_in, rn))
        return [pltpu.make_async_copy(a.at[:, at], b.at[:, at], s_in.at[i, g]) for i, (a, b) in enumerate(pairs)]

    def save(g):
        at = column_span(g, per)
        return pltpu.make_async_copy(out.at[:, at], out_out.at[:, at], s_out.at[g])

    issue(loads(0))
    gather_starts(place, GATHER_THETA, chunked(theta_refs, RING), theta, s_w.at[0], per, LATE_GROUPS)
    gather_starts(place, GATHER_SIGMA, chunked(sigma_refs, RING), sigma, s_w.at[1], per, LATE_GROUPS)
    for g in range(1, LATE_GROUPS):
        issue(loads(g))
    acc[...] = jnp.zeros_like(acc)
    first.wait()

    def group(g, _):
        gather_wait(theta, s_w.at[0], g, per)
        gather_wait(sigma, s_w.at[1], g, per)
        for c in loads(g):
            c.wait()
        for u in range(per):
            n = g * per + u
            at = at_block(n)
            th = block_column(theta, n)
            sg = block_column(sigma, n)
            lhs = jnp.concatenate([tok[:, at_block(rows[n, s])] for s in range(ks)], axis=1)
            mean = jnp.dot(lhs, th, preferred_element_type=f32)
            out[:, at] = (mean + rn[:, at]).astype(bf16)
            for q in range(ks // 2):
                span = slice(q * 2 * LANE, (q + 1) * 2 * LANE)
                one = lax.dot_general(cot[:, at], th[span], NT, preferred_element_type=f32)
                two = lax.dot_general(gv[:, at], sg[span], NT, preferred_element_type=f32)
                for h in range(2):
                    pick = at_block(rows[n, 2 * q + h])
                    p = slice(h * LANE, (h + 1) * LANE)
                    acc[:, pick] += one[:, p] + tok[:, pick].astype(f32) * two[:, p]
        save(g).start()
        return 0

    lax.fori_loop(0, LATE_GROUPS, group, 0)
    w = away_out.shape[2]
    core = place[PLACE["core"]]
    ends = []
    for side, (ref, half) in enumerate(((away_out, 1 - core), (home_out, core))):
        for k in range(RING):
            y = place[PLACE["y"]] ^ k
            both[side, k] = acc[:, pl.ds(pl.multiple_of((y * 2 + half) * w, w), w)].astype(bf16)
            ends.append(pltpu.make_async_copy(both.at[side, k], ref.at[k], s_one.at[1 + side * RING + k]))
            ends[-1].start()
    for c in [save(g) for g in range(LATE_GROUPS)] + ends:
        c.wait()


def late(rows, tok, cot, gv, rn, sigma, theta, own):
    t, d = tok.shape
    ff = cot.shape[1]
    w = d // (2 * RING)
    refs = [r for group in sigma + theta for r in group]
    shapes = [sds((t, ff), bf16), sds((RING, t, w), bf16), sds((RING, t, w), bf16)]
    return pl.pallas_call(
        late_kernel,
        out_shape=shapes,
        in_specs=[SM] + [HB] * (4 + len(refs)),
        out_specs=[HB] * 3,
        scratch_shapes=[
            pltpu.VMEM((t, d), bf16),
            pltpu.VMEM((t, ff), bf16),
            pltpu.VMEM((t, ff), bf16),
            pltpu.VMEM((t, ff), f32),
            pltpu.VMEM((t, ff), bf16),
            pltpu.VMEM((2, RING, t, w), bf16),
            pltpu.VMEM((RING, RING, own, ff), bf16),
            pltpu.VMEM((RING, RING, own, ff), bf16),
            pltpu.VMEM((t, d), f32),
            pltpu.SemaphoreType.DMA((2, LATE_GROUPS)),
            pltpu.SemaphoreType.DMA((3, LATE_GROUPS)),
            pltpu.SemaphoreType.DMA((1 + 2 * RING,)),
            pltpu.SemaphoreType.DMA((LATE_GROUPS,)),
        ],
        compiler_params=PARAMS,
        name="late",
    )(rows, tok, cot, gv, rn, *refs)


def step(tokens, theta, log_sigma2, block_rows, noise, cotangent):
    own = theta.shape[1]
    sg, th = prep(log_sigma2, theta)
    sigma_in = gather(sg, GATHER_SIGMA)
    theta_in = gather(th, GATHER_THETA)
    parts_theta, sq, sqt = early(block_rows, tokens, cotangent, own)
    parts_var, gv, rn = middle(block_rows, sq, sqt, noise, cotangent, sigma_in, own)
    output, away, home = late(block_rows, tokens, cotangent, gv, rn, sigma_in, theta_in, own)
    tokens_all = tokens.shape[0] * lax.axis_size(ROW)
    width = block_rows.shape[1] * LANE
    inv_root = 1.0 / math.sqrt(tokens_all)
    got_theta = scatter(parts_theta, SCATTER_THETA)
    grad_theta = final(got_theta, SCATTER_THETA, theta.shape, inv_root, None)
    got_var = scatter(parts_var, SCATTER_VAR)
    grad_logvar = final(got_var, SCATTER_VAR, theta.shape, 0.5 * width * inv_root, log_sigma2)
    came = sent(away, "core", 1)
    pairs = [(home[k].astype(f32) + came[k].astype(f32)).astype(bf16) for k in range(RING)]
    arrived = steps_sent(pairs, "y")
    grad_tokens = arrived[0].astype(f32)
    for a in arrived[1:]:
        grad_tokens = grad_tokens + a.astype(f32)
    return (output, grad_tokens, grad_theta, grad_logvar)


def solution(mesh):
    finer = Mesh(mesh.devices.reshape(4, 4, 4, 2), ROW + COL)
    in_specs = (P(ROW, None), P(COL, ROW, None), P(COL, ROW, None), P(COL, None), P(ROW, COL), P(ROW, COL))
    out_specs = (P(ROW, COL), P(ROW, COL), P(COL, ROW, None), P(COL, ROW, None))
    return jax.shard_map(step, mesh=finer, in_specs=in_specs, out_specs=out_specs, check_vma=False)
```

```python
import math

import jax
import jax.numpy as jnp
from jax import lax
from jax.experimental import pallas as pl
from jax.experimental.pallas import tpu as pltpu
from jax.sharding import Mesh
from jax.sharding import PartitionSpec as P


ROW = ("z", "x")
COL = ("y", "core")
RING = 4
EPS = 1e-06
LANE = 128
f32, bf16 = jnp.float32, jnp.bfloat16
PARAMS = pltpu.CompilerParams(vmem_limit_bytes=60 * 1024 * 1024)
SM = pl.BlockSpec(memory_space=pltpu.SMEM)
VB = pl.BlockSpec(memory_space=pltpu.VMEM)
HB = pl.BlockSpec(memory_space=pl.ANY)
NT = (((1,), (1,)), ((), ()))

GATHER_SIGMA = (("x", "z", 0, 64),)
GATHER_THETA = (("z", "x", 0, 64),)
SCATTER_THETA = (("x", "z", 0, 64),)
SCATTER_VAR = (("z", "x", 0, 64),)
PLACE = {"z": 0, "x": 1, "y": 2, "core": 3}


def sds(shape, dtype):
    return jax.ShapeDtypeStruct(shape, dtype)


def at_block(index):
    return pl.ds(pl.multiple_of(index * LANE, LANE), LANE)


def sent(value, axis, step):
    n = lax.axis_size(axis)
    return lax.ppermute(value, axis, [(i, (i + step) % n) for i in range(n)])


def steps_of(value, axis):
    return [sent(value, axis, k) for k in range(1, RING)]


def steps_sent(values, axis):
    return [values[0]] + [sent(values[k], axis, k) for k in range(1, RING)]


def prep_kernel(paths_s, paths_t):
    def kernel(ls_ref, theta_ref, *outs):
        for n in range(theta_ref.shape[0]):
            at = slice(n * LANE, (n + 1) * LANE)
            for (_, _, lo, hi), o in zip(paths_s, outs):
                o[:, at] = jnp.exp(ls_ref[n, lo:hi]).astype(bf16)
            for (_, _, lo, hi), o in zip(paths_t, outs[len(paths_s) :]):
                o[:, at] = theta_ref[n, lo:hi]

    return kernel


def prep(ls, theta):
    c, _, b = theta.shape
    shapes = [sds((hi - lo, c * b), bf16) for _, _, lo, hi in GATHER_SIGMA + GATHER_THETA]
    outs = pl.pallas_call(
        prep_kernel(GATHER_SIGMA, GATHER_THETA), out_shape=shapes, compiler_params=PARAMS, name="prep"
    )(ls, theta)
    return outs[: len(GATHER_SIGMA)], outs[len(GATHER_SIGMA) :]


def gather(pieces, paths):
    blocks = [jnp.stack([p] + steps_of(p, path[0])) for p, path in zip(pieces, paths)]
    return [[b] + steps_of(b, path[1]) for b, path in zip(blocks, paths)]


def gather_relayed(piece, path):
    one, two = path[:2]
    block = jnp.stack([piece] + steps_of(piece, one))
    up, down = sent(block, two, 1), sent(block, two, RING - 1)
    far_up, far_down = sent(up[:2], two, 1), sent(down[2:], two, RING - 1)
    return [[block, up, far_up, far_down, down]]


def piece_at(refs, k, j):
    if len(refs) == RING:
        return refs[k].at[j]
    if k == 2:
        return refs[2 + j // 2].at[j % 2]
    return refs[k if k < 2 else 4].at[j]


def chunked(refs, size):
    return [refs[i : i + size] for i in range(0, len(refs), size)]


def block_column(whole, n):
    blk = whole[:, :, :, at_block(n)]
    return blk.reshape(-1, LANE)


def scatter_shapes(paths, ff):
    return [sds((RING, hi - lo, ff), bf16) for _, _, lo, hi in paths for _ in range(RING)]


def summed(arrived, spot):
    total = arrived[0][spot].astype(f32)
    for r in arrived[1:]:
        total = total + r[spot].astype(f32)
    return total.astype(bf16)


def scatter(parts, paths):
    ins = []
    for path, group in zip(paths, chunked(parts, RING)):
        ins += [group[0]] + [sent(group[k], path[0], k) for k in range(1, RING)]
    mid = [summed(group, k) for group in chunked(ins, RING) for k in range(RING)]
    arrived = []
    for path, group in zip(paths, chunked(mid, RING)):
        arrived += [group[0]] + [sent(group[k], path[1], k) for k in range(1, RING)]
    return arrived


def final_kernel(paths, scale, with_sigma):
    def kernel(*refs):
        ls = refs[0] if with_sigma else None
        ins, out = refs[int(with_sigma) : -1], refs[-1]
        for n in range(out.shape[0]):
            at = slice(n * LANE, (n + 1) * LANE)
            for (_, _, lo, hi), group in zip(paths, chunked(ins, RING)):
                total = group[0][:, at].astype(f32)
                for r in group[1:]:
                    total = total + r[:, at].astype(f32)
                if with_sigma:
                    total = total * jnp.exp(ls[n, lo:hi])
                out[n, lo:hi] = total * scale

    return kernel


def final(arrived, paths, shape, scale, ls):
    args = ([] if ls is None else [ls]) + list(arrived)
    return pl.pallas_call(
        final_kernel(paths, scale, ls is not None), out_shape=sds(shape, f32), compiler_params=PARAMS
    )(*args)


EARLY_GROUPS, MIDDLE_GROUPS, LATE_GROUPS = 4, 2, 4
SIGMA_PARTS = 5


def issue(copies):
    for c in copies:
        c.start()


def column_span(group, per):
    w = per * LANE
    return pl.ds(pl.multiple_of(group * w, w), w)


def gather_starts(place, paths, groups, whole, sems, per, count):
    for g in range(count):
        cols = slice(g * per * LANE, (g + 1) * per * LANE)
        for (one, two, lo, hi), refs in zip(paths, groups):
            for k in range(RING):
                for j in range(RING):
                    spot = {one: (place[PLACE[one]] - j) & 3, two: (place[PLACE[two]] - k) & 3}
                    pltpu.make_async_copy(
                        piece_at(refs, k, j).at[:, cols], whole.at[spot["z"], spot["x"], lo:hi, cols], sems.at[g]
                    ).start()


def gather_wait(whole, sems, g, per):
    cols = column_span(g, per)
    part = whole.at[:, :, :, cols]
    pltpu.make_async_copy(part, part, sems.at[g]).wait()


def scatter_start(place, paths, held, groups, sem, cols):
    for (one, two, lo, hi), refs in zip(paths, groups):
        for k in range(RING):
            for j in range(RING):
                spot = {one: (place[PLACE[one]] + k) & 3, two: (place[PLACE[two]] + j) & 3}
                pltpu.make_async_copy(
                    held.at[spot["z"], spot["x"], lo:hi, cols], refs[k].at[j, :, cols], sem
                ).start()


def early_kernel(rows, tok, cot, *refs):
    outs, (sq_out, sqt_out, tokt, held, sq, sqt, sems) = refs[:-7], refs[-7:]
    place = [lax.axis_index(a) for a in ROW + COL]
    blocks = tok.shape[1] // LANE
    ks = rows.shape[1]
    per = cot.shape[1] // LANE // EARLY_GROUPS
    for k in range(blocks):
        at = slice(k * LANE, (k + 1) * LANE)
        wide = tok[:, at].astype(f32)
        sq[:, at] = (wide * wide).astype(bf16)
        turned = tok[:, at].T
        tokt[k] = turned
        wide = turned.astype(f32)
        sqt[k] = (wide * wide).astype(bf16)
    saves = [pltpu.make_async_copy(sq, sq_out, sems.at[0]), pltpu.make_async_copy(sqt, sqt_out, sems.at[1])]
    issue(saves)

    def group(g, _):
        for u in range(per):
            n = g * per + u
            lhs = jnp.concatenate([tokt[rows[n, s]] for s in range(ks)], axis=0)
            part = jnp.dot(lhs, cot[:, at_block(n)], preferred_element_type=f32)
            held[:, :, :, at_block(n)] = part.astype(bf16).reshape(RING, RING, -1, LANE)
        scatter_start(place, SCATTER_THETA, held, chunked(outs, RING), sems.at[2], column_span(g, per))
        return 0

    lax.fori_loop(0, EARLY_GROUPS, group, 0)
    for c in saves:
        c.wait()
    pltpu.make_async_copy(held, held, sems.at[2]).wait()


def early(rows, tok, cot, own):
    t, d = tok.shape
    ff = cot.shape[1]
    shapes = scatter_shapes(SCATTER_THETA, ff) + [sds((t, d), bf16), sds((d // LANE, LANE, t), bf16)]
    outs = pl.pallas_call(
        early_kernel,
        out_shape=shapes,
        in_specs=[SM, VB, VB],
        out_specs=[HB] * len(shapes),
        scratch_shapes=[
            pltpu.VMEM((d // LANE, LANE, t), bf16),
            pltpu.VMEM((RING, RING, own, ff), bf16),
            pltpu.VMEM((t, d), bf16),
            pltpu.VMEM((d // LANE, LANE, t), bf16),
            pltpu.SemaphoreType.DMA((3,)),
        ],
        compiler_params=PARAMS,
        name="early",
    )(rows, tok, cot)
    return outs[:-2], outs[-2], outs[-1]


def middle_kernel(rows, sq_in, sqt_in, noise_in, cot_in, *refs):
    n_in = SIGMA_PARTS
    sigma_refs, outs = refs[:n_in], refs[n_in:-14]
    gv_out, rn_out, sq, sqt, noise, cot, whole, held, gv, rn, s_sig, s_in, s_one, s_out = refs[-14:]
    place = [lax.axis_index(a) for a in ROW + COL]
    ks = rows.shape[1]
    per = noise.shape[1] // LANE // MIDDLE_GROUPS
    first = pltpu.make_async_copy(sq_in, sq, s_one.at[0])
    second = pltpu.make_async_copy(sqt_in, sqt, s_one.at[1])
    first.start()
    gather_starts(place, GATHER_SIGMA, [sigma_refs], whole, s_sig, per, MIDDLE_GROUPS)

    def loads(g):
        at = column_span(g, per)
        return [
            pltpu.make_async_copy(noise_in.at[:, at], noise.at[:, at], s_in.at[0, g]),
            pltpu.make_async_copy(cot_in.at[:, at], cot.at[:, at], s_in.at[1, g]),
        ]

    def saves(g):
        at = column_span(g, per)
        return [
            pltpu.make_async_copy(gv.at[:, at], gv_out.at[:, at], s_out.at[0, g]),
            pltpu.make_async_copy(rn.at[:, at], rn_out.at[:, at], s_out.at[1, g]),
        ]

    issue(loads(0))
    second.start()
    for g in range(1, MIDDLE_GROUPS):
        issue(loads(g))
    first.wait()

    def group(g, _):
        gather_wait(whole, s_sig, g, per)
        for c in loads(g):
            c.wait()
        for u in range(per):
            n = g * per + u
            at = at_block(n)
            lhs = jnp.concatenate([sq[:, at_block(rows[n, s])] for s in range(ks)], axis=1)
            var = jnp.dot(lhs, block_column(whole, n), preferred_element_type=f32) + EPS
            inv = lax.rsqrt(var)
            draw = noise[:, at].astype(f32)
            rn[:, at] = var * inv * draw
            gv[:, at] = (cot[:, at].astype(f32) * draw * inv).astype(bf16)

        @pl.when(g == 0)
        def _():
            second.wait()

        for u in range(per):
            n = g * per + u
            at = at_block(n)
            lhs = jnp.concatenate([sqt[rows[n, s]] for s in range(ks)], axis=0)
            part = jnp.dot(lhs, gv[:, at], preferred_element_type=f32)
            held[:, :, :, at] = part.astype(bf16).reshape(RING, RING, -1, LANE)
        issue(saves(g))
        scatter_start(place, SCATTER_VAR, held, chunked(outs, RING), s_one.at[2], column_span(g, per))
        return 0

    lax.fori_loop(0, MIDDLE_GROUPS, group, 0)
    for g in range(MIDDLE_GROUPS):
        for c in saves(g):
            c.wait()
    pltpu.make_async_copy(held, held, s_one.at[2]).wait()


def middle(rows, sq, sqt, noise, cot, sigma, own):
    t, d = sq.shape
    ff = cot.shape[1]
    shapes = scatter_shapes(SCATTER_VAR, ff) + [sds((t, ff), bf16), sds((t, ff), f32)]
    refs = [r for group in sigma for r in group]
    outs = pl.pallas_call(
        middle_kernel,
        out_shape=shapes,
        in_specs=[SM, HB, HB, HB, HB] + [HB] * len(refs),
        out_specs=[HB] * len(shapes),
        scratch_shapes=[
            pltpu.VMEM((t, d), bf16),
            pltpu.VMEM((d // LANE, LANE, t), bf16),
            pltpu.VMEM((t, ff), bf16),
            pltpu.VMEM((t, ff), bf16),
            pltpu.VMEM((RING, RING, own, ff), bf16),
            pltpu.VMEM((RING, RING, own, ff), bf16),
            pltpu.VMEM((t, ff), bf16),
            pltpu.VMEM((t, ff), f32),
            pltpu.SemaphoreType.DMA((MIDDLE_GROUPS,)),
            pltpu.SemaphoreType.DMA((2, MIDDLE_GROUPS)),
            pltpu.SemaphoreType.DMA((3,)),
            pltpu.SemaphoreType.DMA((2, MIDDLE_GROUPS)),
        ],
        compiler_params=PARAMS,
        name="middle",
    )(rows, sq, sqt, noise, cot, *refs)
    return outs[:-2], outs[-2], outs[-1]


def late_kernel(rows, tok_in, cot_in, gv_in, rn_in, *refs):
    n_s, n_t = SIGMA_PARTS, RING * len(GATHER_THETA)
    sigma_refs, theta_refs = refs[:n_s], refs[n_s : n_s + n_t]
    (out_out, away_out, home_out, tok, cot, gv, rn, out, both, sigma, theta, acc, s_w, s_in, s_one, s_out) = refs[n_s + n_t :]
    place = [lax.axis_index(a) for a in ROW + COL]
    ks = rows.shape[1]
    per = cot.shape[1] // LANE // LATE_GROUPS
    first = pltpu.make_async_copy(tok_in, tok, s_one.at[0])
    first.start()

    def loads(g):
        at = column_span(g, per)
        pairs = ((cot_in, cot), (gv_in, gv), (rn_in, rn))
        return [pltpu.make_async_copy(a.at[:, at], b.at[:, at], s_in.at[i, g]) for i, (a, b) in enumerate(pairs)]

    def save(g):
        at = column_span(g, per)
        return pltpu.make_async_copy(out.at[:, at], out_out.at[:, at], s_out.at[g])

    issue(loads(0))
    gather_starts(place, GATHER_THETA, chunked(theta_refs, RING), theta, s_w.at[0], per, LATE_GROUPS)
    gather_starts(place, GATHER_SIGMA, [sigma_refs], sigma, s_w.at[1], per, LATE_GROUPS)
    for g in range(1, LATE_GROUPS):
        issue(loads(g))
    acc[...] = jnp.zeros_like(acc)
    first.wait()

    def group(g, _):
        gather_wait(theta, s_w.at[0], g, per)
        gather_wait(sigma, s_w.at[1], g, per)
        for c in loads(g):
            c.wait()
        for u in range(per):
            n = g * per + u
            at = at_block(n)
            th = block_column(theta, n)
            sg = block_column(sigma, n)
            lhs = jnp.concatenate([tok[:, at_block(rows[n, s])] for s in range(ks)], axis=1)
            mean = jnp.dot(lhs, th, preferred_element_type=f32)
            out[:, at] = (mean + rn[:, at]).astype(bf16)
            for q in range(ks // 2):
                span = slice(q * 2 * LANE, (q + 1) * 2 * LANE)
                one = lax.dot_general(cot[:, at], th[span], NT, preferred_element_type=f32)
                two = lax.dot_general(gv[:, at], sg[span], NT, preferred_element_type=f32)
                for h in range(2):
                    pick = at_block(rows[n, 2 * q + h])
                    p = slice(h * LANE, (h + 1) * LANE)
                    acc[:, pick] += one[:, p] + tok[:, pick].astype(f32) * two[:, p]
        save(g).start()
        return 0

    lax.fori_loop(0, LATE_GROUPS, group, 0)
    w = away_out.shape[2]
    core = place[PLACE["core"]]
    ends = []
    for side, (ref, half) in enumerate(((away_out, 1 - core), (home_out, core))):
        for k in range(RING):
            y = (place[PLACE["y"]] + k) & 3
            both[side, k] = acc[:, pl.ds(pl.multiple_of((y * 2 + half) * w, w), w)].astype(bf16)
            ends.append(pltpu.make_async_copy(both.at[side, k], ref.at[k], s_one.at[1 + side * RING + k]))
            ends[-1].start()
    for c in [save(g) for g in range(LATE_GROUPS)] + ends:
        c.wait()


def late(rows, tok, cot, gv, rn, sigma, theta, own):
    t, d = tok.shape
    ff = cot.shape[1]
    w = d // (2 * RING)
    refs = [r for group in sigma + theta for r in group]
    shapes = [sds((t, ff), bf16), sds((RING, t, w), bf16), sds((RING, t, w), bf16)]
    return pl.pallas_call(
        late_kernel,
        out_shape=shapes,
        in_specs=[SM] + [HB] * (4 + len(refs)),
        out_specs=[HB] * 3,
        scratch_shapes=[
            pltpu.VMEM((t, d), bf16),
            pltpu.VMEM((t, ff), bf16),
            pltpu.VMEM((t, ff), bf16),
            pltpu.VMEM((t, ff), f32),
            pltpu.VMEM((t, ff), bf16),
            pltpu.VMEM((2, RING, t, w), bf16),
            pltpu.VMEM((RING, RING, own, ff), bf16),
            pltpu.VMEM((RING, RING, own, ff), bf16),
            pltpu.VMEM((t, d), f32),
            pltpu.SemaphoreType.DMA((2, LATE_GROUPS)),
            pltpu.SemaphoreType.DMA((3, LATE_GROUPS)),
            pltpu.SemaphoreType.DMA((1 + 2 * RING,)),
            pltpu.SemaphoreType.DMA((LATE_GROUPS,)),
        ],
        compiler_params=PARAMS,
        name="late",
    )(rows, tok, cot, gv, rn, *refs)


def step(tokens, theta, log_sigma2, block_rows, noise, cotangent):
    own = theta.shape[1]
    sg, th = prep(log_sigma2, theta)
    sigma_in = gather_relayed(sg[0], GATHER_SIGMA[0])
    theta_in = gather(th, GATHER_THETA)
    parts_theta, sq, sqt = early(block_rows, tokens, cotangent, own)
    parts_var, gv, rn = middle(block_rows, sq, sqt, noise, cotangent, sigma_in, own)
    output, away, home = late(block_rows, tokens, cotangent, gv, rn, sigma_in, theta_in, own)
    tokens_all = tokens.shape[0] * lax.axis_size(ROW)
    width = block_rows.shape[1] * LANE
    inv_root = 1.0 / math.sqrt(tokens_all)
    got_theta = scatter(parts_theta, SCATTER_THETA)
    grad_theta = final(got_theta, SCATTER_THETA, theta.shape, inv_root, None)
    got_var = scatter(parts_var, SCATTER_VAR)
    grad_logvar = final(got_var, SCATTER_VAR, theta.shape, 0.5 * width * inv_root, log_sigma2)
    came = sent(away, "core", 1)
    pairs = [(home[k].astype(f32) + came[k].astype(f32)).astype(bf16) for k in range(RING)]
    pairs = lax.optimization_barrier(pairs)
    arrived = steps_sent(pairs, "y")
    grad_tokens = arrived[0].astype(f32)
    for a in arrived[1:]:
        grad_tokens = grad_tokens + a.astype(f32)
    return (output, grad_tokens, grad_theta, grad_logvar)


def solution(mesh):
    finer = Mesh(mesh.devices.reshape(4, 4, 4, 2), ROW + COL)
    in_specs = (P(ROW, None), P(COL, ROW, None), P(COL, ROW, None), P(COL, None), P(ROW, COL), P(ROW, COL))
    out_specs = (P(ROW, COL), P(ROW, COL), P(COL, ROW, None), P(COL, ROW, None))
    return jax.shard_map(step, mesh=finer, in_specs=in_specs, out_specs=out_specs, check_vma=False)
```

```python
import math

import jax
import jax.numpy as jnp
from jax import lax
from jax.experimental import pallas as pl
from jax.experimental.pallas import tpu as pltpu
from jax.sharding import Mesh
from jax.sharding import PartitionSpec as P


ROW = ("z", "x")
COL = ("y", "core")
RING = 4
EPS = 1e-06
LANE = 128
f32, bf16 = jnp.float32, jnp.bfloat16
PARAMS = pltpu.CompilerParams(vmem_limit_bytes=60 * 1024 * 1024)
SM = pl.BlockSpec(memory_space=pltpu.SMEM)
VB = pl.BlockSpec(memory_space=pltpu.VMEM)
HB = pl.BlockSpec(memory_space=pl.ANY)
NT = (((1,), (1,)), ((), ()))

GATHER_SIGMA = (("x", "z"),)
GATHER_THETA = (("z", "x"),)
SCATTER_THETA = (("x", "z"),)
SCATTER_VAR = (("z", "x"),)
PLACE = {"z": 0, "x": 1, "y": 2, "core": 3}


def sds(shape, dtype):
    return jax.ShapeDtypeStruct(shape, dtype)


def at_block(index):
    return pl.ds(pl.multiple_of(index * LANE, LANE), LANE)


def sent(value, axis, step):
    n = lax.axis_size(axis)
    return lax.ppermute(value, axis, [(i, (i + step) % n) for i in range(n)])


def steps_of(value, axis):
    return [sent(value, axis, k) for k in range(1, RING)]


def steps_sent(values, axis):
    return [values[0]] + [sent(values[k], axis, k) for k in range(1, RING)]


def gather(pieces, paths):
    blocks = [jnp.stack([p] + steps_of(p, path[0])) for p, path in zip(pieces, paths)]
    return [[b] + steps_of(b, path[1]) for b, path in zip(blocks, paths)]


def gather_relayed(piece, path):
    one, two = path[:2]
    block = jnp.stack([piece] + steps_of(piece, one))
    up, down = sent(block, two, 1), sent(block, two, RING - 1)
    far_up, far_down = sent(up[:2], two, 1), sent(down[2:], two, RING - 1)
    return [[block, up, far_up, far_down, down]]


def piece_at(refs, k, j):
    if len(refs) == RING:
        return refs[k].at[j]
    if k == 2:
        return refs[2 + j // 2].at[j % 2]
    return refs[k if k < 2 else 4].at[j]


def chunked(refs, size):
    return [refs[i : i + size] for i in range(0, len(refs), size)]


def block_column(whole, n):
    return whole[n].reshape(-1, LANE)


def scatter_shapes(paths, columns, own):
    return [sds((RING, columns, own, LANE), bf16) for _ in paths for _ in range(RING)]


def summed(arrived, spot):
    total = arrived[0][spot].astype(f32)
    for r in arrived[1:]:
        total = total + r[spot].astype(f32)
    return total.astype(bf16)


def scatter(parts, paths):
    ins = []
    for path, group in zip(paths, chunked(parts, RING)):
        ins += [group[0]] + [sent(group[k], path[0], k) for k in range(1, RING)]
    mid = [summed(group, k) for group in chunked(ins, RING) for k in range(RING)]
    arrived = []
    for path, group in zip(paths, chunked(mid, RING)):
        arrived += [group[0]] + [sent(group[k], path[1], k) for k in range(1, RING)]
    return arrived


def total_of(arrived):
    total = arrived[0].astype(f32)
    for a in arrived[1:]:
        total = total + a.astype(f32)
    return total


EARLY_GROUPS, MIDDLE_GROUPS, LATE_GROUPS = 4, 2, 4
SIGMA_PARTS = 5


def issue(copies):
    for c in copies:
        c.start()


def column_span(group, per):
    w = per * LANE
    return pl.ds(pl.multiple_of(group * w, w), w)


def gather_starts(place, paths, groups, whole, sems, per, count):
    for g in range(count):
        cols = slice(g * per, (g + 1) * per)
        for (one, two), refs in zip(paths, groups):
            for k in range(RING):
                for j in range(RING):
                    spot = {one: (place[PLACE[one]] - j) & 3, two: (place[PLACE[two]] - k) & 3}
                    pltpu.make_async_copy(
                        piece_at(refs, k, j).at[cols], whole.at[cols, spot["z"], spot["x"]], sems.at[g]
                    ).start()


def gather_wait(whole, sems, g, per):
    part = whole.at[pl.ds(g * per, per)]
    pltpu.make_async_copy(part, part, sems.at[g]).wait()


def scatter_start(place, paths, held, groups, sem, cols):
    for (one, two), refs in zip(paths, groups):
        for k in range(RING):
            for j in range(RING):
                spot = {one: (place[PLACE[one]] + k) & 3, two: (place[PLACE[two]] + j) & 3}
                pltpu.make_async_copy(
                    held.at[cols, spot["z"], spot["x"]], refs[k].at[j, cols], sem
                ).start()


def early_kernel(rows, tok, cot, *refs):
    outs, (sq_out, sqt_out, tokt, held, sq, sqt, sems) = refs[:-7], refs[-7:]
    place = [lax.axis_index(a) for a in ROW + COL]
    blocks = tok.shape[1] // LANE
    ks = rows.shape[0]
    per = cot.shape[1] // LANE // EARLY_GROUPS
    for k in range(blocks):
        at = slice(k * LANE, (k + 1) * LANE)
        wide = tok[:, at].astype(f32)
        sq[:, at] = (wide * wide).astype(bf16)
        turned = tok[:, at].T
        tokt[k] = turned
        wide = turned.astype(f32)
        sqt[k] = (wide * wide).astype(bf16)
    saves = [pltpu.make_async_copy(sq, sq_out, sems.at[0]), pltpu.make_async_copy(sqt, sqt_out, sems.at[1])]
    issue(saves)

    def group(g, _):
        for u in range(per):
            n = g * per + u
            lhs = jnp.concatenate([tokt[rows[s, n]] for s in range(ks)], axis=0)
            part = jnp.dot(lhs, cot[:, at_block(n)], preferred_element_type=f32)
            held[n] = part.astype(bf16).reshape(RING, RING, -1, LANE)
        scatter_start(place, SCATTER_THETA, held, chunked(outs, RING), sems.at[2], pl.ds(g * per, per))
        return 0

    lax.fori_loop(0, EARLY_GROUPS, group, 0)
    for c in saves:
        c.wait()
    pltpu.make_async_copy(held, held, sems.at[2]).wait()


def early(rows, tok, cot, own):
    t, d = tok.shape
    ff = cot.shape[1]
    shapes = scatter_shapes(SCATTER_THETA, ff // LANE, own) + [sds((t, d), bf16), sds((d // LANE, LANE, t), bf16)]
    outs = pl.pallas_call(
        early_kernel,
        out_shape=shapes,
        in_specs=[SM, VB, VB],
        out_specs=[HB] * len(shapes),
        scratch_shapes=[
            pltpu.VMEM((d // LANE, LANE, t), bf16),
            pltpu.VMEM((ff // LANE, RING, RING, own, LANE), bf16),
            pltpu.VMEM((t, d), bf16),
            pltpu.VMEM((d // LANE, LANE, t), bf16),
            pltpu.SemaphoreType.DMA((3,)),
        ],
        compiler_params=PARAMS,
        name="early",
    )(rows, tok, cot)
    return outs[:-2], outs[-2], outs[-1]


def middle_kernel(rows, sq_in, sqt_in, noise_in, cot_in, *refs):
    n_in = SIGMA_PARTS
    sigma_refs, outs = refs[:n_in], refs[n_in:-14]
    gv_out, rn_out, sq, sqt, noise, cot, whole, held, gv, rn, s_sig, s_in, s_one, s_out = refs[-14:]
    place = [lax.axis_index(a) for a in ROW + COL]
    ks = rows.shape[0]
    per = noise.shape[1] // LANE // MIDDLE_GROUPS
    first = pltpu.make_async_copy(sq_in, sq, s_one.at[0])
    second = pltpu.make_async_copy(sqt_in, sqt, s_one.at[1])
    first.start()
    gather_starts(place, GATHER_SIGMA, [sigma_refs], whole, s_sig, per, MIDDLE_GROUPS)

    def loads(g):
        at = column_span(g, per)
        return [
            pltpu.make_async_copy(noise_in.at[:, at], noise.at[:, at], s_in.at[0, g]),
            pltpu.make_async_copy(cot_in.at[:, at], cot.at[:, at], s_in.at[1, g]),
        ]

    def saves(g):
        at = column_span(g, per)
        return [
            pltpu.make_async_copy(gv.at[:, at], gv_out.at[:, at], s_out.at[0, g]),
            pltpu.make_async_copy(rn.at[:, at], rn_out.at[:, at], s_out.at[1, g]),
        ]

    issue(loads(0))
    second.start()
    for g in range(1, MIDDLE_GROUPS):
        issue(loads(g))
    first.wait()

    def group(g, _):
        gather_wait(whole, s_sig, g, per)
        for c in loads(g):
            c.wait()
        for u in range(per):
            n = g * per + u
            at = at_block(n)
            lhs = jnp.concatenate([sq[:, at_block(rows[s, n])] for s in range(ks)], axis=1)
            var = jnp.dot(lhs, block_column(whole, n), preferred_element_type=f32) + EPS
            inv = lax.rsqrt(var)
            draw = noise[:, at].astype(f32)
            rn[:, at] = var * inv * draw
            gv[:, at] = (cot[:, at].astype(f32) * draw * inv).astype(bf16)

        @pl.when(g == 0)
        def _():
            second.wait()

        for u in range(per):
            n = g * per + u
            at = at_block(n)
            lhs = jnp.concatenate([sqt[rows[s, n]] for s in range(ks)], axis=0)
            part = jnp.dot(lhs, gv[:, at], preferred_element_type=f32)
            held[n] = part.astype(bf16).reshape(RING, RING, -1, LANE)
        issue(saves(g))
        scatter_start(place, SCATTER_VAR, held, chunked(outs, RING), s_one.at[2], pl.ds(g * per, per))
        return 0

    lax.fori_loop(0, MIDDLE_GROUPS, group, 0)
    for g in range(MIDDLE_GROUPS):
        for c in saves(g):
            c.wait()
    pltpu.make_async_copy(held, held, s_one.at[2]).wait()


def middle(rows, sq, sqt, noise, cot, sigma, own):
    t, d = sq.shape
    ff = cot.shape[1]
    shapes = scatter_shapes(SCATTER_VAR, ff // LANE, own) + [sds((t, ff), bf16), sds((t, ff), f32)]
    refs = [r for group in sigma for r in group]
    outs = pl.pallas_call(
        middle_kernel,
        out_shape=shapes,
        in_specs=[SM, HB, HB, HB, HB] + [HB] * len(refs),
        out_specs=[HB] * len(shapes),
        scratch_shapes=[
            pltpu.VMEM((t, d), bf16),
            pltpu.VMEM((d // LANE, LANE, t), bf16),
            pltpu.VMEM((t, ff), bf16),
            pltpu.VMEM((t, ff), bf16),
            pltpu.VMEM((ff // LANE, RING, RING, own, LANE), bf16),
            pltpu.VMEM((ff // LANE, RING, RING, own, LANE), bf16),
            pltpu.VMEM((t, ff), bf16),
            pltpu.VMEM((t, ff), f32),
            pltpu.SemaphoreType.DMA((MIDDLE_GROUPS,)),
            pltpu.SemaphoreType.DMA((2, MIDDLE_GROUPS)),
            pltpu.SemaphoreType.DMA((3,)),
            pltpu.SemaphoreType.DMA((2, MIDDLE_GROUPS)),
        ],
        compiler_params=PARAMS,
        name="middle",
    )(rows, sq, sqt, noise, cot, *refs)
    return outs[:-2], outs[-2], outs[-1]


def late_kernel(rows, tok_in, cot_in, gv_in, rn_in, *refs):
    n_s, n_t = SIGMA_PARTS, RING * len(GATHER_THETA)
    sigma_refs, theta_refs = refs[:n_s], refs[n_s : n_s + n_t]
    (out_out, away_out, home_out, tok, cot, gv, rn, out, both, sigma, theta, acc, s_w, s_in, s_one, s_out) = refs[n_s + n_t :]
    place = [lax.axis_index(a) for a in ROW + COL]
    ks = rows.shape[0]
    per = cot.shape[1] // LANE // LATE_GROUPS
    first = pltpu.make_async_copy(tok_in, tok, s_one.at[0])
    first.start()

    def loads(g):
        at = column_span(g, per)
        pairs = ((cot_in, cot), (gv_in, gv), (rn_in, rn))
        return [pltpu.make_async_copy(a.at[:, at], b.at[:, at], s_in.at[i, g]) for i, (a, b) in enumerate(pairs)]

    def save(g):
        at = column_span(g, per)
        return pltpu.make_async_copy(out.at[:, at], out_out.at[:, at], s_out.at[g])

    issue(loads(0))
    gather_starts(place, GATHER_THETA, chunked(theta_refs, RING), theta, s_w.at[0], per, LATE_GROUPS)
    gather_starts(place, GATHER_SIGMA, [sigma_refs], sigma, s_w.at[1], per, LATE_GROUPS)
    for g in range(1, LATE_GROUPS):
        issue(loads(g))
    acc[...] = jnp.zeros_like(acc)
    first.wait()

    def group(g, _):
        gather_wait(theta, s_w.at[0], g, per)
        gather_wait(sigma, s_w.at[1], g, per)
        for c in loads(g):
            c.wait()
        for u in range(per):
            n = g * per + u
            at = at_block(n)
            th = block_column(theta, n)
            sg = block_column(sigma, n)
            lhs = jnp.concatenate([tok[:, at_block(rows[s, n])] for s in range(ks)], axis=1)
            mean = jnp.dot(lhs, th, preferred_element_type=f32)
            out[:, at] = (mean + rn[:, at]).astype(bf16)
            part_rows = tok.shape[0] // 4
            for q in range(ks // 2):
                span = slice(q * 2 * LANE, (q + 1) * 2 * LANE)
                for m in range(4):
                    r = slice(m * part_rows, (m + 1) * part_rows)
                    one = lax.dot_general(cot[r, at], th[span], NT, preferred_element_type=f32)
                    two = lax.dot_general(gv[r, at], sg[span], NT, preferred_element_type=f32)
                    for h in range(2):
                        pick = at_block(rows[2 * q + h, n])
                        p = slice(h * LANE, (h + 1) * LANE)
                        acc[r, pick] += one[:, p] + tok[r, pick].astype(f32) * two[:, p]
        save(g).start()
        return 0

    lax.fori_loop(0, LATE_GROUPS, group, 0)
    w = away_out.shape[2]
    core = place[PLACE["core"]]
    ends = []
    for side, (ref, half) in enumerate(((away_out, 1 - core), (home_out, core))):
        for k in range(RING):
            y = (place[PLACE["y"]] + k) & 3
            both[side, k] = acc[:, pl.ds(pl.multiple_of((y * 2 + half) * w, w), w)].astype(bf16)
            ends.append(pltpu.make_async_copy(both.at[side, k], ref.at[k], s_one.at[1 + side * RING + k]))
            ends[-1].start()
    for c in [save(g) for g in range(LATE_GROUPS)] + ends:
        c.wait()


def late(rows, tok, cot, gv, rn, sigma, theta, own):
    t, d = tok.shape
    ff = cot.shape[1]
    w = d // (2 * RING)
    refs = [r for group in sigma + theta for r in group]
    shapes = [sds((t, ff), bf16), sds((RING, t, w), bf16), sds((RING, t, w), bf16)]
    return pl.pallas_call(
        late_kernel,
        out_shape=shapes,
        in_specs=[SM] + [HB] * (4 + len(refs)),
        out_specs=[HB] * 3,
        scratch_shapes=[
            pltpu.VMEM((t, d), bf16),
            pltpu.VMEM((t, ff), bf16),
            pltpu.VMEM((t, ff), bf16),
            pltpu.VMEM((t, ff), f32),
            pltpu.VMEM((t, ff), bf16),
            pltpu.VMEM((2, RING, t, w), bf16),
            pltpu.VMEM((ff // LANE, RING, RING, own, LANE), bf16),
            pltpu.VMEM((ff // LANE, RING, RING, own, LANE), bf16),
            pltpu.VMEM((t, d), f32),
            pltpu.SemaphoreType.DMA((2, LATE_GROUPS)),
            pltpu.SemaphoreType.DMA((3, LATE_GROUPS)),
            pltpu.SemaphoreType.DMA((1 + 2 * RING,)),
            pltpu.SemaphoreType.DMA((LATE_GROUPS,)),
        ],
        compiler_params=PARAMS,
        name="late",
    )(rows, tok, cot, gv, rn, *refs)


def step(tokens, theta, log_sigma2, block_rows, noise, cotangent):
    own = theta.shape[1]
    width = block_rows.shape[1] * LANE
    rows = block_rows.T
    sg, th = [jnp.exp(log_sigma2).astype(bf16)], [theta]
    sigma_in = gather_relayed(sg[0], GATHER_SIGMA[0])
    theta_in = gather(th, GATHER_THETA)
    parts_theta, sq, sqt = early(rows, tokens, cotangent, own)
    parts_var, gv, rn = middle(rows, sq, sqt, noise, cotangent, sigma_in, own)
    output, away, home = late(rows, tokens, cotangent, gv, rn, sigma_in, theta_in, own)
    tokens_all = tokens.shape[0] * lax.axis_size(ROW)
    inv_root = 1.0 / math.sqrt(tokens_all)
    got_theta = scatter(parts_theta, SCATTER_THETA)
    grad_theta = total_of(got_theta) * inv_root
    got_var = scatter(parts_var, SCATTER_VAR)
    grad_logvar = jnp.exp(log_sigma2) * total_of(got_var) * (0.5 * width * inv_root)
    came = sent(away, "core", 1)
    pairs = [(home[k].astype(f32) + came[k].astype(f32)).astype(bf16) for k in range(RING)]
    pairs = lax.optimization_barrier(pairs)
    arrived = steps_sent(pairs, "y")
    grad_tokens = total_of(arrived)
    return (output, grad_tokens, grad_theta, grad_logvar)


def solution(mesh):
    finer = Mesh(mesh.devices.reshape(4, 4, 4, 2), ROW + COL)
    in_specs = (P(ROW, None), P(COL, ROW, None), P(COL, ROW, None), P(COL, None), P(ROW, COL), P(ROW, COL))
    out_specs = (P(ROW, COL), P(ROW, COL), P(COL, ROW, None), P(COL, ROW, None))
    return jax.shard_map(step, mesh=finer, in_specs=in_specs, out_specs=out_specs, check_vma=False)
```

```python
import math

import jax
import jax.numpy as jnp
from jax import lax
from jax.experimental import pallas as pl
from jax.experimental.pallas import tpu as pltpu
from jax.sharding import Mesh
from jax.sharding import PartitionSpec as P


ROW = ("z", "x")
COL = ("y", "core")
RING = 4
EPS = 1e-06
LANE = 128
f32, bf16 = jnp.float32, jnp.bfloat16
PARAMS = pltpu.CompilerParams(vmem_limit_bytes=60 * 1024 * 1024)
SM = pl.BlockSpec(memory_space=pltpu.SMEM)
VB = pl.BlockSpec(memory_space=pltpu.VMEM)
HB = pl.BlockSpec(memory_space=pl.ANY)
NT = (((1,), (1,)), ((), ()))

GATHER_SIGMA = (("x", "z"),)
GATHER_THETA = (("z", "x"),)
SCATTER_THETA = (("x", "z"),)
SCATTER_VAR = (("z", "x"),)
PLACE = {"z": 0, "x": 1, "y": 2, "core": 3}


def sds(shape, dtype):
    return jax.ShapeDtypeStruct(shape, dtype)


def at_block(index):
    return pl.ds(pl.multiple_of(index * LANE, LANE), LANE)


def sent(value, axis, step):
    n = lax.axis_size(axis)
    return lax.ppermute(value, axis, [(i, (i + step) % n) for i in range(n)])


def steps_of(value, axis):
    return [sent(value, axis, k) for k in range(1, RING)]


def gather(pieces, paths):
    blocks = [jnp.stack([p] + steps_of(p, path[0])) for p, path in zip(pieces, paths)]
    return [[b] + steps_of(b, path[1]) for b, path in zip(blocks, paths)]


def gather_relayed(piece, path):
    one, two = path[:2]
    block = jnp.stack([piece] + steps_of(piece, one))
    up, down = sent(block, two, 1), sent(block, two, RING - 1)
    far_up, far_down = sent(up[:2], two, 1), sent(down[2:], two, RING - 1)
    return [[block, up, far_up, far_down, down]]


def piece_at(refs, k, j):
    if len(refs) == RING:
        return refs[k].at[j]
    if k == 2:
        return refs[2 + j // 2].at[j % 2]
    return refs[k if k < 2 else 4].at[j]


def chunked(refs, size):
    return [refs[i : i + size] for i in range(0, len(refs), size)]


def block_column(whole, n):
    return whole[n].reshape(-1, LANE)


def scatter_shapes(paths, columns, own):
    return [sds((RING, columns, own, LANE), bf16) for _ in paths for _ in range(RING)]


def summed(arrived, spot):
    total = arrived[0][spot].astype(f32)
    for r in arrived[1:]:
        total = total + r[spot].astype(f32)
    return total.astype(bf16)


def scatter(parts, paths):
    ins = []
    for path, group in zip(paths, chunked(parts, RING)):
        ins += [group[0]] + [sent(group[k], path[0], k) for k in range(1, RING)]
    mid = [summed(group, k) for group in chunked(ins, RING) for k in range(RING)]
    arrived = []
    for path, group in zip(paths, chunked(mid, RING)):
        arrived += [group[0]] + [sent(group[k], path[1], k) for k in range(1, RING)]
    return arrived


def total_of(arrived):
    total = arrived[0].astype(f32)
    for a in arrived[1:]:
        total = total + a.astype(f32)
    return total


EARLY_GROUPS, MIDDLE_GROUPS, LATE_GROUPS = 4, 2, 4
SIGMA_PARTS = 5
SLOTS = ((0, 0), (2, 1), (1, 3), (3, 2))


def issue(copies):
    for c in copies:
        c.start()


def column_span(group, per):
    w = per * LANE
    return pl.ds(pl.multiple_of(group * w, w), w)


def gather_starts(place, paths, groups, whole, sems, per, count):
    for g in range(count):
        cols = slice(g * per, (g + 1) * per)
        for (one, two), refs in zip(paths, groups):
            for k in range(RING):
                for j in range(RING):
                    spot = {one: (place[PLACE[one]] - j) & 3, two: (place[PLACE[two]] - k) & 3}
                    pltpu.make_async_copy(
                        piece_at(refs, k, j).at[cols], whole.at[cols, spot["z"], spot["x"]], sems.at[g]
                    ).start()


def gather_wait(whole, sems, g, per):
    part = whole.at[pl.ds(g * per, per)]
    pltpu.make_async_copy(part, part, sems.at[g]).wait()


def scatter_start(place, paths, held, groups, sem, cols):
    for (one, two), refs in zip(paths, groups):
        for k in range(RING):
            for j in range(RING):
                spot = {one: (place[PLACE[one]] + k) & 3, two: (place[PLACE[two]] + j) & 3}
                pltpu.make_async_copy(
                    held.at[cols, spot["z"], spot["x"]], refs[k].at[j, cols], sem
                ).start()


def early_kernel(rows, tok, cot, *refs):
    outs, (sq_out, sqt_out, tokt, held, sq, sqt, sems) = refs[:-7], refs[-7:]
    place = [lax.axis_index(a) for a in ROW + COL]
    blocks = tok.shape[1] // LANE
    ks = rows.shape[0]
    per = cot.shape[1] // LANE // EARLY_GROUPS
    for k in range(blocks):
        at = slice(k * LANE, (k + 1) * LANE)
        wide = tok[:, at].astype(f32)
        sq[:, at] = (wide * wide).astype(bf16)
        turned = tok[:, at].T
        tokt[k] = turned
        wide = turned.astype(f32)
        sqt[k] = (wide * wide).astype(bf16)
    saves = [pltpu.make_async_copy(sq, sq_out, sems.at[0]), pltpu.make_async_copy(sqt, sqt_out, sems.at[1])]
    issue(saves)

    def group(g, _):
        for u in range(per):
            n = g * per + u
            lhs = jnp.concatenate([tokt[rows[s, n]] for s in range(ks)], axis=0)
            part = jnp.dot(lhs, cot[:, at_block(n)], preferred_element_type=f32)
            held[n] = part.astype(bf16).reshape(RING, RING, -1, LANE)
        scatter_start(place, SCATTER_THETA, held, chunked(outs, RING), sems.at[2], pl.ds(g * per, per))
        return 0

    lax.fori_loop(0, EARLY_GROUPS, group, 0)
    for c in saves:
        c.wait()
    pltpu.make_async_copy(held, held, sems.at[2]).wait()


def early(rows, tok, cot, own):
    t, d = tok.shape
    ff = cot.shape[1]
    shapes = scatter_shapes(SCATTER_THETA, ff // LANE, own) + [sds((t, d), bf16), sds((d // LANE, LANE, t), bf16)]
    outs = pl.pallas_call(
        early_kernel,
        out_shape=shapes,
        in_specs=[SM, VB, VB],
        out_specs=[HB] * len(shapes),
        scratch_shapes=[
            pltpu.VMEM((d // LANE, LANE, t), bf16),
            pltpu.VMEM((ff // LANE, RING, RING, own, LANE), bf16),
            pltpu.VMEM((t, d), bf16),
            pltpu.VMEM((d // LANE, LANE, t), bf16),
            pltpu.SemaphoreType.DMA((3,)),
        ],
        compiler_params=PARAMS,
        name="early",
    )(rows, tok, cot)
    return outs[:-2], outs[-2], outs[-1]


def middle_kernel(rows, sq_in, sqt_in, noise_in, cot_in, *refs):
    n_in = SIGMA_PARTS
    sigma_refs, outs = refs[:n_in], refs[n_in:-14]
    gv_out, rn_out, sq, sqt, noise, cot, whole, held, gv, rn, s_sig, s_in, s_one, s_out = refs[-14:]
    place = [lax.axis_index(a) for a in ROW + COL]
    ks = rows.shape[0]
    per = noise.shape[1] // LANE // MIDDLE_GROUPS
    first = pltpu.make_async_copy(sq_in, sq, s_one.at[0])
    second = pltpu.make_async_copy(sqt_in, sqt, s_one.at[1])
    first.start()
    gather_starts(place, GATHER_SIGMA, [sigma_refs], whole, s_sig, per, MIDDLE_GROUPS)

    def loads(g):
        at = column_span(g, per)
        return [
            pltpu.make_async_copy(noise_in.at[:, at], noise.at[:, at], s_in.at[0, g]),
            pltpu.make_async_copy(cot_in.at[:, at], cot.at[:, at], s_in.at[1, g]),
        ]

    def saves(g):
        at = column_span(g, per)
        return [
            pltpu.make_async_copy(gv.at[:, at], gv_out.at[:, at], s_out.at[0, g]),
            pltpu.make_async_copy(rn.at[:, at], rn_out.at[:, at], s_out.at[1, g]),
        ]

    issue(loads(0))
    second.start()
    for g in range(1, MIDDLE_GROUPS):
        issue(loads(g))
    first.wait()

    def group(g, _):
        gather_wait(whole, s_sig, g, per)
        for c in loads(g):
            c.wait()
        for u in range(per):
            n = g * per + u
            at = at_block(n)
            lhs = jnp.concatenate([sq[:, at_block(rows[s, n])] for s in range(ks)], axis=1)
            var = jnp.dot(lhs, block_column(whole, n), preferred_element_type=f32) + EPS
            inv = lax.rsqrt(var)
            draw = noise[:, at].astype(f32)
            rn[:, at] = var * inv * draw
            gv[:, at] = (cot[:, at].astype(f32) * draw * inv).astype(bf16)

        @pl.when(g == 0)
        def _():
            second.wait()

        for u in range(per):
            n = g * per + u
            at = at_block(n)
            lhs = jnp.concatenate([sqt[rows[s, n]] for s in range(ks)], axis=0)
            part = jnp.dot(lhs, gv[:, at], preferred_element_type=f32)
            held[n] = part.astype(bf16).reshape(RING, RING, -1, LANE)
        issue(saves(g))
        scatter_start(place, SCATTER_VAR, held, chunked(outs, RING), s_one.at[2], pl.ds(g * per, per))
        return 0

    lax.fori_loop(0, MIDDLE_GROUPS, group, 0)
    for g in range(MIDDLE_GROUPS):
        for c in saves(g):
            c.wait()
    pltpu.make_async_copy(held, held, s_one.at[2]).wait()


def middle(rows, sq, sqt, noise, cot, sigma, own):
    t, d = sq.shape
    ff = cot.shape[1]
    shapes = scatter_shapes(SCATTER_VAR, ff // LANE, own) + [sds((t, ff), bf16), sds((t, ff), f32)]
    refs = [r for group in sigma for r in group]
    outs = pl.pallas_call(
        middle_kernel,
        out_shape=shapes,
        in_specs=[SM, HB, HB, HB, HB] + [HB] * len(refs),
        out_specs=[HB] * len(shapes),
        scratch_shapes=[
            pltpu.VMEM((t, d), bf16),
            pltpu.VMEM((d // LANE, LANE, t), bf16),
            pltpu.VMEM((t, ff), bf16),
            pltpu.VMEM((t, ff), bf16),
            pltpu.VMEM((ff // LANE, RING, RING, own, LANE), bf16),
            pltpu.VMEM((ff // LANE, RING, RING, own, LANE), bf16),
            pltpu.VMEM((t, ff), bf16),
            pltpu.VMEM((t, ff), f32),
            pltpu.SemaphoreType.DMA((MIDDLE_GROUPS,)),
            pltpu.SemaphoreType.DMA((2, MIDDLE_GROUPS)),
            pltpu.SemaphoreType.DMA((3,)),
            pltpu.SemaphoreType.DMA((2, MIDDLE_GROUPS)),
        ],
        compiler_params=PARAMS,
        name="middle",
    )(rows, sq, sqt, noise, cot, *refs)
    return outs[:-2], outs[-2], outs[-1]


def late_kernel(rows, tok_in, cot_in, gv_in, rn_in, *refs):
    n_s, n_t = SIGMA_PARTS, RING * len(GATHER_THETA)
    sigma_refs, theta_refs = refs[:n_s], refs[n_s : n_s + n_t]
    (out_out, away_out, home_out, tok, cot, gv, rn, out, both, sigma, theta, acc, s_w, s_in, s_one, s_out) = refs[n_s + n_t :]
    place = [lax.axis_index(a) for a in ROW + COL]
    ks = rows.shape[0]
    per = cot.shape[1] // LANE // LATE_GROUPS
    first = pltpu.make_async_copy(tok_in, tok, s_one.at[0])
    first.start()

    def loads(g):
        at = column_span(g, per)
        pairs = ((cot_in, cot), (gv_in, gv), (rn_in, rn))
        return [pltpu.make_async_copy(a.at[:, at], b.at[:, at], s_in.at[i, g]) for i, (a, b) in enumerate(pairs)]

    def save(g):
        at = column_span(g, per)
        return pltpu.make_async_copy(out.at[:, at], out_out.at[:, at], s_out.at[g])

    issue(loads(0))
    gather_starts(place, GATHER_THETA, chunked(theta_refs, RING), theta, s_w.at[0], per, LATE_GROUPS)
    gather_starts(place, GATHER_SIGMA, [sigma_refs], sigma, s_w.at[1], per, LATE_GROUPS)
    for g in range(1, LATE_GROUPS):
        issue(loads(g))
    acc[...] = jnp.zeros_like(acc)
    first.wait()

    def group(g, _):
        gather_wait(theta, s_w.at[0], g, per)
        gather_wait(sigma, s_w.at[1], g, per)
        for c in loads(g):
            c.wait()
        for u in range(per):
            n = g * per + u
            at = at_block(n)
            th = block_column(theta, n)
            sg = block_column(sigma, n)
            lhs = jnp.concatenate([tok[:, at_block(rows[s, n])] for s in range(ks)], axis=1)
            mean = jnp.dot(lhs, th, preferred_element_type=f32)
            out[:, at] = (mean + rn[:, at]).astype(bf16)
            part_rows = tok.shape[0] // 4
            for q in range(ks // 2):
                span = slice(q * 2 * LANE, (q + 1) * 2 * LANE)
                for m in range(4):
                    r = slice(m * part_rows, (m + 1) * part_rows)
                    one = lax.dot_general(cot[r, at], th[span], NT, preferred_element_type=f32)
                    two = lax.dot_general(gv[r, at], sg[span], NT, preferred_element_type=f32)
                    for h in range(2):
                        pick = at_block(rows[2 * q + h, n])
                        p = slice(h * LANE, (h + 1) * LANE)
                        acc[r, pick] += one[:, p] + tok[r, pick].astype(f32) * two[:, p]
        save(g).start()
        return 0

    lax.fori_loop(0, LATE_GROUPS, group, 0)
    w = away_out.shape[2]
    core = place[PLACE["core"]]
    ends = []
    mid = tok.shape[0] // 2
    for side, (ref, half) in enumerate(((away_out, 1 - core), (home_out, core))):
        for k in range(RING):
            y = (place[PLACE["y"]] + k) & 3
            both[side, k] = acc[:, pl.ds(pl.multiple_of((y * 2 + half) * w, w), w)].astype(bf16)
            for slot in range(RING):
                for part in range(2):
                    if SLOTS[slot][part] == k:
                        r = slice(part * mid, (part + 1) * mid)
                        pltpu.make_async_copy(both.at[side, k, r], ref.at[slot, r], s_one.at[1 + side]).start()
        ends.append(pltpu.make_async_copy(both.at[side], both.at[side], s_one.at[1 + side]))
    for c in [save(g) for g in range(LATE_GROUPS)] + ends:
        c.wait()


def late(rows, tok, cot, gv, rn, sigma, theta, own):
    t, d = tok.shape
    ff = cot.shape[1]
    w = d // (2 * RING)
    refs = [r for group in sigma + theta for r in group]
    shapes = [sds((t, ff), bf16), sds((RING, t, w), bf16), sds((RING, t, w), bf16)]
    return pl.pallas_call(
        late_kernel,
        out_shape=shapes,
        in_specs=[SM] + [HB] * (4 + len(refs)),
        out_specs=[HB] * 3,
        scratch_shapes=[
            pltpu.VMEM((t, d), bf16),
            pltpu.VMEM((t, ff), bf16),
            pltpu.VMEM((t, ff), bf16),
            pltpu.VMEM((t, ff), f32),
            pltpu.VMEM((t, ff), bf16),
            pltpu.VMEM((2, RING, t, w), bf16),
            pltpu.VMEM((ff // LANE, RING, RING, own, LANE), bf16),
            pltpu.VMEM((ff // LANE, RING, RING, own, LANE), bf16),
            pltpu.VMEM((t, d), f32),
            pltpu.SemaphoreType.DMA((2, LATE_GROUPS)),
            pltpu.SemaphoreType.DMA((3, LATE_GROUPS)),
            pltpu.SemaphoreType.DMA((1 + 2 * RING,)),
            pltpu.SemaphoreType.DMA((LATE_GROUPS,)),
        ],
        compiler_params=PARAMS,
        name="late",
    )(rows, tok, cot, gv, rn, *refs)


def step(tokens, theta, log_sigma2, block_rows, noise, cotangent):
    own = theta.shape[1]
    width = block_rows.shape[1] * LANE
    rows = block_rows.T
    sg, th = [jnp.exp(log_sigma2).astype(bf16)], [theta]
    sigma_in = gather_relayed(sg[0], GATHER_SIGMA[0])
    theta_in = gather(th, GATHER_THETA)
    parts_theta, sq, sqt = early(rows, tokens, cotangent, own)
    parts_var, gv, rn = middle(rows, sq, sqt, noise, cotangent, sigma_in, own)
    output, away, home = late(rows, tokens, cotangent, gv, rn, sigma_in, theta_in, own)
    tokens_all = tokens.shape[0] * lax.axis_size(ROW)
    inv_root = 1.0 / math.sqrt(tokens_all)
    got_theta = scatter(parts_theta, SCATTER_THETA)
    grad_theta = total_of(got_theta) * inv_root
    got_var = scatter(parts_var, SCATTER_VAR)
    grad_logvar = jnp.exp(log_sigma2) * total_of(got_var) * (0.5 * width * inv_root)
    came = sent(away, "core", 1)
    pairs = [(home[k].astype(f32) + came[k].astype(f32)).astype(bf16) for k in range(RING)]
    pairs = lax.optimization_barrier(pairs)
    mid = home.shape[1] // 2
    below, above = sent(pairs[1], "y", 1), sent(pairs[3], "y", RING - 1)
    up = (pairs[2][:mid].astype(f32) + below[:mid].astype(f32)).astype(bf16)
    down = (pairs[2][mid:].astype(f32) + above[mid:].astype(f32)).astype(bf16)
    below_far, above_far = sent(up, "y", 1), sent(down, "y", RING - 1)
    top = total_of([pairs[0][:mid], below_far, above[:mid]])
    bottom = total_of([pairs[0][mid:], below[mid:], above_far])
    grad_tokens = jnp.concatenate([top, bottom], axis=0)
    return (output, grad_tokens, grad_theta, grad_logvar)


def solution(mesh):
    finer = Mesh(mesh.devices.reshape(4, 4, 4, 2), ROW + COL)
    in_specs = (P(ROW, None), P(COL, ROW, None), P(COL, ROW, None), P(COL, None), P(ROW, COL), P(ROW, COL))
    out_specs = (P(ROW, COL), P(ROW, COL), P(COL, ROW, None), P(COL, ROW, None))
    return jax.shard_map(step, mesh=finer, in_specs=in_specs, out_specs=out_specs, check_vma=False)
```
